128 devices in a mesh: gx: 8 (over x, core), gy: 16 (over z, y).
Axes of the slice: x: 4, y: 4, z: 4, core: 2. Of those that a mesh axis runs over, the one named last changes fastest.
Arguments:
- positions: float32 [3, 16, 32, 8, 128], P(None, 'gx', 'gy'), may hold values from 0 to 1, as said below
- velocities: float32 [3, 16, 32, 8, 128], P(None, 'gx', 'gy'), may hold values from -6 to 6
- kicks: float32 [3, 16, 32, 8, 128], P(None, 'gx', 'gy'), may hold values from -6 to 6
- counts: int32 [16, 32, 8], P('gx', 'gy'), may hold values from 64 to 128, as said below
- subcell: int32 [16, 32, 8, 128], P('gx', 'gy'), may hold values from 0 to 26, as said below
- electron_temp: float32 [48, 96, 24], P('gx', 'gy'), may hold values from 1 to 2
- laser_flux: float32 [48, 96], P('gx', 'gy'), may hold values from 1 to 10
Outputs:
- next_velocities: float32 [3, 16, 32, 8, 128], P(None, 'gx', 'gy')
- next_temperature: float32 [48, 96, 24], P('gx', 'gy')
The draws below stay inside these ranges and needn't reach their ends.
Inputs may be any that keep to these rules, and one draw needn't show every extreme that they name: `counts`: at least one tile holds exactly 128 live atoms. subcell = 9 a + 3 b + c for the atom's grid cell offsets a, b, c along x, y, z within its tile. `positions`: each component lies in the grid cell named by subcell: component x in [a/3, (a+1)/3), likewise y with b and z with c.
All inputs are finite; a program needn't handle non-finite values.
Results may differ from the reference program's by a relative error of at most 0.0003.
Values sent between devices are 32-bit elements; how exact they have to be, the bound alone decides.
A program may use at most 128 MiB of HBM per device.

```python
import math
import jax
import jax.numpy as jnp
from jax import lax

SLOTS = 128
TZ = 8
TILES_X = 16
TILES_Y = 32


def draw_cells(key):
    return jax.random.randint(jax.random.fold_in(key, 1), (TILES_X, TILES_Y, TZ, SLOTS), 0, 27, dtype=jnp.int32)


def draw_subcell(key, part):
    return draw_cells(key)


def draw_positions(key, part):
    cells = draw_cells(key)
    fraction = jax.random.uniform(jax.random.fold_in(key, 2), (3, TILES_X, TILES_Y, TZ, SLOTS), jnp.float32)
    corner = jnp.stack([cells // 9, cells // 3 % 3, cells % 3]).astype(jnp.float32)
    return (corner + fraction) / 3.0


def draw_counts(key, part):
    number = TILES_X * TILES_Y * TZ
    filled = jax.random.randint(jax.random.fold_in(key, 3), (number,), SLOTS // 2, SLOTS + 1, dtype=jnp.int32)
    chosen = jax.random.randint(jax.random.fold_in(key, 4), (), 0, number, dtype=jnp.int32)
    places = jnp.arange(number, dtype=jnp.int32)
    filled = jnp.where(places == chosen, jnp.int32(SLOTS), filled)
    return filled.reshape(TILES_X, TILES_Y, TZ)


def level_of(key, extent, shards, low, top_value):
    def one(axis_at, shards_of):
        steps = jax.random.uniform(jax.random.fold_in(jax.random.fold_in(key, 6), axis_at), (shards_of,), jnp.float32, low / len(shards), top_value / len(shards))
        return jnp.repeat(jnp.exp(steps), extent[axis_at] // shards_of).reshape((-1,) + (1,) * (len(extent) - axis_at - 1))

    gain = one(*shards[0])
    for cut in shards[1:]:
        gain = gain * one(*cut)
    return gain


def bell_draw(stream_key, extent, deviation, reach, cuts=(), kind=jnp.bfloat16):
    entries = deviation * jax.random.normal(stream_key, extent, jnp.float32)
    if cuts:
        entries = entries * level_of(stream_key, extent, cuts, -0.22, 0.18)
    return jnp.clip(entries, -reach, reach).astype(kind)


def setup_inputs(seed: int = 0) -> dict:
    seeds = jax.random.split(jax.random.key(seed), 8)
    return {
        "positions": draw_positions(jax.random.fold_in(seeds[7], 71), 0),
        "velocities": bell_draw(seeds[1], (3, TILES_X, TILES_Y, TZ, SLOTS), 1.0, 6.0, ((1, 8), (2, 16)), jnp.float32),
        "kicks": bell_draw(seeds[2], (3, TILES_X, TILES_Y, TZ, SLOTS), 1.0, 6.0, ((1, 8), (2, 16)), jnp.float32),
        "counts": draw_counts(jax.random.fold_in(seeds[7], 71), 0),
        "subcell": draw_subcell(jax.random.fold_in(seeds[7], 71), 0),
        "electron_temp": jnp.clip(1.0 + 1.0 * jax.random.uniform(seeds[5], (3 * TILES_X, 3 * TILES_Y, 3 * TZ), jnp.float32) ** level_of(seeds[5], (3 * TILES_X, 3 * TILES_Y, 3 * TZ), ((0, 8), (1, 16)), -0.2, 0.2), 1.0, 2.0),
        "laser_flux": jnp.clip(jnp.exp(math.log(10.0) - 2.3025851 * jax.random.uniform(seeds[6], (3 * TILES_X, 3 * TILES_Y), jnp.float32) ** level_of(seeds[6], (3 * TILES_X, 3 * TILES_Y), ((0, 8), (1, 16)), -0.2, 0.2)), 1.0, 10.0),
    }


far_away = 1000.0
cutoff_sq = 0.2
pair_scale = 0.3
time_step = 0.1
friction = 1.0
heat_capacity = 40.0
conduct = 0.05
laser_gain = 0.05
absorb_depth = 38.0

def neighbour_offsets():
    return [(shift_x, shift_y, shift_z) for shift_x in (-1, 0, 1) for shift_y in (-1, 0, 1) for shift_z in (-1, 0, 1)]

def displacement(centre, neighbour, shift_x, shift_y, shift_z):
    offset = jnp.array([shift_x, shift_y, shift_z], jnp.float32)
    return centre[:, :, :, None] - neighbour[:, :, None, :] - offset[:, None, None, None]

def density(padded, centre_x, centre_y):
    depth = padded.shape[3] - 2
    centre = padded[:, centre_x, centre_y, 1:depth + 1]
    total = jnp.zeros(centre.shape[1:], jnp.float32)
    for shift_x, shift_y, shift_z in neighbour_offsets():
        neighbour = padded[:, centre_x + shift_x, centre_y + shift_y, 1 + shift_z:1 + shift_z + depth]
        displace = displacement(centre, neighbour, shift_x, shift_y, shift_z)
        scaled = lax.optimization_barrier(jnp.sum(displace * displace, axis=0)) / cutoff_sq
        weight = jnp.maximum(1.0 - scaled, 0.0)
        total = total + lax.optimization_barrier(jnp.sum(weight * weight * weight, axis=-1))
    return total - 1.0

def embed_slope(rho):
    return -0.5 / jnp.sqrt(1.0 + rho)

def forces(padded, slopes, centre_x, centre_y):
    depth = padded.shape[3] - 2
    centre = padded[:, centre_x, centre_y, 1:depth + 1]
    own_slope = slopes[centre_x, centre_y, 1:depth + 1]
    total = jnp.zeros(centre.shape, jnp.float32)
    for shift_x, shift_y, shift_z in neighbour_offsets():
        neighbour = padded[:, centre_x + shift_x, centre_y + shift_y, 1 + shift_z:1 + shift_z + depth]
        other_slope = slopes[centre_x + shift_x, centre_y + shift_y, 1 + shift_z:1 + shift_z + depth]
        displace = displacement(centre, neighbour, shift_x, shift_y, shift_z)
        scaled = lax.optimization_barrier(jnp.sum(displace * displace, axis=0)) / cutoff_sq
        weight = jnp.maximum(1.0 - scaled, 0.0)
        square = weight * weight
        pair_term = pair_scale * (-3.0 * square * (1.0 - 2.0 * scaled) - 2.0 * square * weight)
        dens_term = -3.0 * square
        factor = (pair_term + (own_slope[:, :, None] + other_slope[:, None, :]) * dens_term) * (2.0 / cutoff_sq)
        total = total - lax.optimization_barrier(jnp.sum(factor[None] * displace, axis=-1))
    return total

def cells_of_grid(grid, tiles_x, tiles_y, depth):
    return grid.reshape(tiles_x, 3, tiles_y, 3, depth, 3).transpose(0, 2, 4, 1, 3, 5).reshape(tiles_x, tiles_y, depth, 27)

def grid_of_cells(cells, tiles_x, tiles_y, depth):
    return cells.reshape(tiles_x, tiles_y, depth, 3, 3, 3).transpose(0, 3, 1, 4, 2, 5).reshape(3 * tiles_x, 3 * tiles_y, 3 * depth)

def atom_update(force, velocities, kicks, live, subcell, electron_temp, laser_flux):
    tiles_x, tiles_y, depth, slots = subcell.shape
    te_cells = cells_of_grid(electron_temp, tiles_x, tiles_y, depth)
    cell_ids = lax.broadcasted_iota(jnp.int32, (27, 1), 0)
    onehot = (subcell[..., None, :] == cell_ids).astype(jnp.float32)
    te_atom = lax.optimization_barrier(jnp.sum(onehot * te_cells[..., None], axis=-2))
    sigma = jnp.sqrt(2.0 * friction * time_step * te_atom)
    moved = velocities + time_step * (force - friction * velocities) + sigma[None] * kicks
    new_vel = jnp.where(live[None], moved, 0.0)
    work = time_step * friction * lax.optimization_barrier(jnp.sum(velocities * velocities, axis=0)) - sigma * lax.optimization_barrier(jnp.sum(kicks * velocities, axis=0))
    work = jnp.where(live, work, 0.0)
    gained = lax.optimization_barrier(jnp.sum(onehot * work[..., None, :], axis=-1))
    grid_gain = grid_of_cells(gained, tiles_x, tiles_y, depth)
    height = lax.broadcasted_iota(jnp.float32, (1, 1, 3 * depth), 2)
    source = laser_gain * laser_flux[:, :, None] * jnp.exp(-(height + 0.5) / absorb_depth)
    heated = electron_temp + grid_gain / heat_capacity + source
    return (new_vel, heated)

def diffuse_padded(padded):
    centre = padded[1:-1, 1:-1]
    lateral = conduct * 0.5 * (centre + padded[:-2, 1:-1]) * (padded[:-2, 1:-1] - centre)
    lateral = lateral + conduct * 0.5 * (centre + padded[2:, 1:-1]) * (padded[2:, 1:-1] - centre)
    lateral = lateral + conduct * 0.5 * (centre + padded[1:-1, :-2]) * (padded[1:-1, :-2] - centre)
    lateral = lateral + conduct * 0.5 * (centre + padded[1:-1, 2:]) * (padded[1:-1, 2:] - centre)
    vertical = conduct * 0.5 * (centre[:, :, 1:] + centre[:, :, :-1]) * (centre[:, :, 1:] - centre[:, :, :-1])
    zflux = jnp.pad(vertical, ((0, 0), (0, 0), (0, 1))) - jnp.pad(vertical, ((0, 0), (0, 0), (1, 0)))
    return centre + lateral + zflux

def reference(positions, velocities, kicks, counts, subcell, electron_temp, laser_flux):
    slot_ids = lax.broadcasted_iota(jnp.int32, (1, 1, 1, SLOTS), 3)
    live = slot_ids < counts[..., None]
    placed = jnp.where(live[None], positions, far_away)
    wrapped = jnp.pad(placed, ((0, 0), (1, 1), (1, 1), (0, 0), (0, 0)), mode='wrap')
    padded = jnp.pad(wrapped, ((0, 0), (0, 0), (0, 0), (1, 1), (0, 0)), constant_values=far_away)
    columns = jnp.arange(TILES_X * TILES_Y, dtype=jnp.int32)
    zero = jnp.int32(0)

    def rho_column(flat_index):
        column_x = flat_index // TILES_Y
        column_y = flat_index % TILES_Y
        neighbourhood = lax.dynamic_slice(padded, (zero, column_x, column_y, zero, zero), (3, 3, 3, TZ + 2, SLOTS))
        return density(neighbourhood, 1, 1)
    rho = lax.map(rho_column, columns).reshape(TILES_X, TILES_Y, TZ, SLOTS)
    slopes = embed_slope(rho)
    slope_wrap = jnp.pad(slopes, ((1, 1), (1, 1), (0, 0), (0, 0)), mode='wrap')
    slope_pad = jnp.pad(slope_wrap, ((0, 0), (0, 0), (1, 1), (0, 0)))

    def force_column(flat_index):
        column_x = flat_index // TILES_Y
        column_y = flat_index % TILES_Y
        neighbourhood = lax.dynamic_slice(padded, (zero, column_x, column_y, zero, zero), (3, 3, 3, TZ + 2, SLOTS))
        slope_piece = lax.dynamic_slice(slope_pad, (column_x, column_y, zero, zero), (3, 3, TZ + 2, SLOTS))
        return forces(neighbourhood, slope_piece, 1, 1)
    force = lax.map(force_column, columns).reshape(TILES_X, TILES_Y, 3, TZ, SLOTS).transpose(2, 0, 1, 3, 4)
    new_vel, heated = atom_update(force, velocities, kicks, live, subcell, electron_temp, laser_flux)
    temper = heated
    for substep in range(3):
        temper = diffuse_padded(jnp.pad(temper, ((1, 1), (1, 1), (0, 0)), mode='wrap'))
    return (new_vel, temper)
```

```python
import jax
import jax.numpy as jnp
import numpy as np
from jax import lax
from jax.experimental import pallas as pl
from jax.experimental.pallas import tpu as pltpu
from jax.sharding import PartitionSpec as P

far_away = 1000.0
cutoff_sq = 0.2
pair_scale = 0.3
time_step = 0.1
friction = 1.0
heat_capacity = 40.0
conduct = 0.05
laser_gain = 0.05
absorb_depth = 38.0


def with_halo(cells, sides, width):
    for axis, dim in sides:
        count = lax.axis_size(axis)
        head = lax.slice_in_dim(cells, 0, width, axis=dim)
        tail = lax.slice_in_dim(cells, cells.shape[dim] - width, cells.shape[dim], axis=dim)
        cells = jnp.concatenate(
            [
                lax.ppermute(tail, axis, [(i, (i + 1) % count) for i in range(count)]),
                cells,
                lax.ppermute(head, axis, [((i + 1) % count, i) for i in range(count)]),
            ],
            axis=dim,
        )
    return cells


def cells_of_grid(grid, tiles_x, tiles_y, depth):
    return (
        grid.reshape(tiles_x, 3, tiles_y, 3, depth, 3)
        .transpose(0, 2, 4, 1, 3, 5)
        .reshape(tiles_x, tiles_y, depth, 27)
    )


def grid_of_cells(cells, tiles_x, tiles_y, depth):
    return (
        cells.reshape(tiles_x, tiles_y, depth, 3, 3, 3)
        .transpose(0, 3, 1, 4, 2, 5)
        .reshape(3 * tiles_x, 3 * tiles_y, 3 * depth)
    )


def atom_update(force, velocities, kicks, live, subcell, electron_temp, laser_flux):
    tiles_x, tiles_y, depth, slots = subcell.shape
    te_cells = cells_of_grid(electron_temp, tiles_x, tiles_y, depth)
    cell_ids = lax.broadcasted_iota(jnp.int32, (27, 1), 0)
    onehot = (subcell[..., None, :] == cell_ids).astype(jnp.float32)
    te_atom = jnp.sum(onehot * te_cells[..., None], axis=-2)
    sigma = jnp.sqrt(2.0 * friction * time_step * te_atom)
    moved = velocities + time_step * (force - friction * velocities) + sigma[None] * kicks
    new_vel = jnp.where(live[None], moved, 0.0)
    work = time_step * friction * jnp.sum(velocities * velocities, axis=0) - sigma * jnp.sum(
        kicks * velocities, axis=0
    )
    work = jnp.where(live, work, 0.0)
    gained = jnp.sum(onehot * work[..., None, :], axis=-1)
    grid_gain = grid_of_cells(gained, tiles_x, tiles_y, depth)
    height = lax.broadcasted_iota(jnp.float32, (1, 1, 3 * depth), 2)
    source = laser_gain * laser_flux[:, :, None] * jnp.exp(-(height + 0.5) / absorb_depth)
    heated = electron_temp + grid_gain / heat_capacity + source
    return (new_vel, heated)


def diffuse_padded(padded):
    centre = padded[1:-1, 1:-1]
    lateral = conduct * 0.5 * (centre + padded[:-2, 1:-1]) * (padded[:-2, 1:-1] - centre)
    lateral = lateral + conduct * 0.5 * (centre + padded[2:, 1:-1]) * (padded[2:, 1:-1] - centre)
    lateral = lateral + conduct * 0.5 * (centre + padded[1:-1, :-2]) * (padded[1:-1, :-2] - centre)
    lateral = lateral + conduct * 0.5 * (centre + padded[1:-1, 2:]) * (padded[1:-1, 2:] - centre)
    vertical = (
        conduct
        * 0.5
        * (centre[:, :, 1:] + centre[:, :, :-1])
        * (centre[:, :, 1:] - centre[:, :, :-1])
    )
    zflux = jnp.pad(vertical, ((0, 0), (0, 0), (0, 1))) - jnp.pad(
        vertical, ((0, 0), (0, 0), (1, 0))
    )
    return centre + lateral + zflux


ROOT = float(np.sqrt(5.0))
ROWS = 4096 + 64
TILES = 32
RANK_KEY = 1024
FAST = 24


def static_tables():
    keys = []
    for t in range(TILES):
        x, y, z = t // 16, t // 8 % 2, t % 8
        for o in range(8):
            ox, oy, oz = o // 4, o // 2 % 2, o % 2
            keys.append((((x + ox) * 3 + (y + oy)) * 9 + z + oz, t * 8 + o))
    order = [k[1] for k in sorted(keys)]
    rank = np.zeros(256, np.int64)
    rank[order] = np.arange(256)
    before = (rank[None, :] < rank[:, None]).astype(np.float32)
    vertex = np.array([k[0] for k in keys])
    start = (vertex[None, :] < np.arange(82)[:, None]).astype(np.float32)
    return np.array(order, np.int32), before, start


def expand_rows(order_s, base_s, count_s, widest, feats, key_ref, outs):
    sub = lax.broadcasted_iota(jnp.int32, (8, 128), 0)

    def chunk(item, tile, octant, k):
        key = key_ref[pl.ds(tile, 8, stride=0), :]
        hit = key == sub + (octant * RANK_KEY + k * 8)
        row = base_s[item] + k * 8
        for n, out in enumerate(outs):
            value = feats(tile, n)
            total = jnp.sum(jnp.where(hit, value, 0.0), axis=1, keepdims=True)
            out[pl.ds(row, 8), :] = jnp.broadcast_to(total, (8, 128))

    @pl.when(widest <= FAST)
    def _():
        def step(i, carry):
            for u in range(4):
                item = order_s[i * 4 + u]
                for k in range(FAST // 8):
                    chunk(item, item // 8, item % 8, k)
            return carry

        lax.fori_loop(0, 64, step, 0)

    @pl.when(widest > FAST)
    def _():
        def step(i, carry):
            item = order_s[i]

            def inner(k, c):
                chunk(item, item // 8, item % 8, k)
                return c

            return lax.fori_loop(0, (count_s[item] + 7) // 8, inner, carry)

        lax.fori_loop(0, 256, step, 0)


def own_tile(tile):
    return (tile // 16 + 1) * 40 + (tile // 8 % 2 + 1) * 10 + tile % 8 + 1


def over_vertices(start_s, body):
    def column(c, carry):
        def level(z, carry):
            v = c * 9 + z
            first, last = start_s[v], start_s[v + 1]
            low = (c // 3) * 40 + (c % 3) * 10 + z

            def block(b, carry):
                body(first + b * 16, low)
                return carry

            return lax.fori_loop(0, (last - first + 15) // 16, block, carry)

        return lax.fori_loop(0, 9, level, carry)

    lax.fori_loop(0, 9, column, 0)


def around(low):
    return [low + dx * 40 + dy * 10 + dz for dx in (0, 1) for dy in (0, 1) for dz in (0, 1)]


def density_kernel(order_s, base_s, count_s, start_s, widest_s, jf, key, xi, yi, zi, ti, tl, acc):
    widest = widest_s[0]

    def feats(tile, n):
        return jf[own_tile(tile), pl.ds(n, 8, stride=0), :]

    expand_rows(order_s, base_s, count_s, widest, feats, key, (xi, yi, zi))

    def body(row, low):
        x2, y2, z2, aa, tot = [], [], [], [], []
        for k in range(2):
            x, y, z = (r[pl.ds(row + 8 * k, 8), :] for r in (xi, yi, zi))
            aa.append(1.0 - (x * x + y * y + z * z))
            x2.append(x + x)
            y2.append(y + y)
            z2.append(z + z)
            tot.append(None)
        for tile in around(low):
            xj, yj, zj, bj = (jf[tile, pl.ds(n, 8, stride=0), :] for n in range(4))
            for k in range(2):
                w = (aa[k] + bj) + (x2[k] * xj + y2[k] * yj + z2[k] * zj)
                w = jnp.maximum(w, 0.0)
                cube = w * w * w
                tot[k] = cube if tot[k] is None else tot[k] + cube
        for k in range(2):
            acc[pl.ds(row + 8 * k, 8), :] = tot[k]

    over_vertices(start_s, body)

    sub = lax.broadcasted_iota(jnp.int32, (8, 128), 0)

    def finish(tile, octant, k, lanes):
        row = base_s[tile * 8 + octant] + k * 8
        tot = jnp.sum(acc[pl.ds(row, 8), :], axis=1, keepdims=True)
        t = jnp.broadcast_to(0.1875 + 0.625 * lax.rsqrt(tot), (8, 128))
        hit = key[pl.ds(tile, 8, stride=0), :] == sub + (octant * RANK_KEY + k * 8)
        return row, t, lanes + jnp.where(hit, t, 0.0)

    @pl.when(widest <= FAST)
    def _():
        def step(tile, carry):
            lanes = jnp.zeros((8, 128), jnp.float32)
            for octant in range(8):
                for k in range(FAST // 8):
                    _, _, lanes = finish(tile, octant, k, lanes)
            tl[pl.ds(tile, 1), :] = jnp.sum(lanes, axis=0, keepdims=True)
            return carry

        lax.fori_loop(0, TILES, step, 0)

    @pl.when(widest > FAST)
    def _():
        def step(tile, carry):
            def per(octant, lanes):
                def inner(k, lanes):
                    return finish(tile, octant, k, lanes)[2]

                return lax.fori_loop(0, (count_s[tile * 8 + octant] + 7) // 8, inner, lanes)

            lanes = lax.fori_loop(0, 8, per, jnp.zeros((8, 128), jnp.float32))
            tl[pl.ds(tile, 1), :] = jnp.sum(lanes, axis=0, keepdims=True)
            return carry

        lax.fori_loop(0, TILES, step, 0)

    def rows(i, carry):
        for k in range(8):
            r = pl.multiple_of(i * 64, 64) + k * 8
            tot = jnp.sum(acc[pl.ds(r, 8), :], axis=1, keepdims=True)
            ti[pl.ds(r, 8), :] = jnp.broadcast_to(0.1875 + 0.625 * lax.rsqrt(tot), (8, 128))
        return carry

    lax.fori_loop(0, (start_s[81] + 63) // 64, rows, 0)


def force_kernel(base_s, count_s, start_s, widest_s, jf, tj, key, xi, yi, zi, ti, out, fx, fy, fz):
    widest = widest_s[0]

    def body(row, low):
        own = [[r[pl.ds(row + 8 * k, 8), :] for r in (xi, yi, zi, ti)] for k in range(2)]
        tot = [[None] * 3, [None] * 3]
        for tile in around(low):
            other = [jf[tile, pl.ds(n, 8, stride=0), :] for n in range(3)]
            t_other = tj[pl.ds(tile, 8, stride=0), :]
            for k in range(2):
                d = [own[k][n] - other[n] for n in range(3)]
                w = jnp.maximum(1.0 - (d[0] * d[0] + d[1] * d[1] + d[2] * d[2]), 0.0)
                g = (w * w) * ((own[k][3] + t_other) - w)
                for n in range(3):
                    p = g * d[n]
                    tot[k][n] = p if tot[k][n] is None else tot[k][n] + p
        for k in range(2):
            for n, f in enumerate((fx, fy, fz)):
                f[pl.ds(row + 8 * k, 8), :] = tot[k][n]

    over_vertices(start_s, body)

    sub = lax.broadcasted_iota(jnp.int32, (8, 128), 0)

    def finish(tile, octant, k, lanes):
        row = base_s[tile * 8 + octant] + k * 8
        hit = key[pl.ds(tile, 8, stride=0), :] == sub + (octant * RANK_KEY + k * 8)
        new = []
        for n, f in enumerate((fx, fy, fz)):
            tot = jnp.sum(f[pl.ds(row, 8), :], axis=1, keepdims=True)
            new.append(lanes[n] + jnp.where(hit, tot, 0.0))
        return tuple(new)

    zero = jnp.zeros((8, 128), jnp.float32)

    def put(tile, lanes):
        for n in range(3):
            out[n, pl.ds(tile, 1), :] = jnp.sum(lanes[n], axis=0, keepdims=True) * (-24.0 / ROOT)

    @pl.when(widest <= FAST)
    def _():
        def step(tile, carry):
            lanes = (zero, zero, zero)
            for octant in range(8):
                for k in range(FAST // 8):
                    lanes = finish(tile, octant, k, lanes)
            put(tile, lanes)
            return carry

        lax.fori_loop(0, TILES, step, 0)

    @pl.when(widest > FAST)
    def _():
        def step(tile, carry):
            def per(octant, lanes):
                def inner(k, lanes):
                    return finish(tile, octant, k, lanes)

                return lax.fori_loop(0, (count_s[tile * 8 + octant] + 7) // 8, inner, lanes)

            put(tile, lax.fori_loop(0, 8, per, (zero, zero, zero)))
            return carry

        lax.fori_loop(0, TILES, step, 0)


VMEM = pl.BlockSpec(memory_space=pltpu.VMEM)
SMEM = pl.BlockSpec(memory_space=pltpu.SMEM)
PARAMS = pltpu.CompilerParams(vmem_limit_bytes=60 << 20)


def plan(positions, live):
    order, before, start = static_tables()
    half = [(positions[n] >= 0.5).astype(jnp.int32) for n in range(3)]
    octant = (half[0] * 4 + half[1] * 2 + half[2]).reshape(TILES, 128)
    alive = live.reshape(TILES, 128)
    hot = ((octant[:, None, :] == jnp.arange(8)[None, :, None]) & alive[:, None, :]).astype(jnp.float32)
    upper = jnp.asarray(np.triu(np.ones((128, 128), np.float32)))
    upto = jnp.dot(hot.reshape(256, 128), upper)
    count = upto[:, 127]
    rank = jnp.sum(hot * upto.reshape(TILES, 8, 128), axis=1).astype(jnp.int32) - 1
    key = jnp.where(alive, octant * RANK_KEY + rank, -1)
    base = jnp.dot(jnp.asarray(before), count).astype(jnp.int32)
    first = jnp.dot(jnp.asarray(start), count).astype(jnp.int32)
    count = count.astype(jnp.int32)
    return jnp.asarray(order), base, count, first, jnp.max(count).reshape(1), key


def film_pad(cycle):
    return jnp.pad(cycle, ((0, 0), (0, 0), (0, 0), (1, 1), (0, 0)), constant_values=far_away)


def local(positions, velocities, kicks, counts, subcell, electron_temp, laser_flux):
    slots = positions.shape[-1]
    depth = positions.shape[3]
    slot_ids = lax.broadcasted_iota(jnp.int32, (1, 1, depth, slots), 3)
    live = slot_ids < counts[..., None]
    placed = jnp.where(live[None], positions, far_away)
    order, base, count, first, widest, key = plan(positions, live)
    padded = film_pad(with_halo(placed, (("gx", 1), ("gy", 2)), 1))
    shift = [
        (np.arange(4) - 2.0).reshape(4, 1, 1, 1),
        (np.arange(4) - 2.0).reshape(1, 4, 1, 1),
        (np.arange(10) - 5.0).reshape(1, 1, 10, 1),
    ]
    xyz = [((padded[n] + jnp.asarray(shift[n], jnp.float32)) * ROOT).reshape(160, 128) for n in range(3)]
    norm = -(xyz[0] * xyz[0] + xyz[1] * xyz[1] + xyz[2] * xyz[2])
    jf = jnp.stack(xyz + [norm] * 5, axis=1)
    row = jax.ShapeDtypeStruct((ROWS, 128), jnp.float32)
    xi, yi, zi, ti, tl = pl.pallas_call(
        density_kernel,
        name="density",
        out_shape=(row, row, row, row, jax.ShapeDtypeStruct((TILES, 128), jnp.float32)),
        in_specs=[SMEM] * 5 + [VMEM] * 2,
        out_specs=(VMEM,) * 5,
        scratch_shapes=[pltpu.VMEM((ROWS, 128), jnp.float32)],
        compiler_params=PARAMS,
    )(order, base, count, first, widest, jf, key)
    t_cycle = with_halo(tl.reshape(2, 2, 8, 128), (("gx", 0), ("gy", 1)), 1)
    tj = jnp.pad(t_cycle, ((0, 0), (0, 0), (1, 1), (0, 0))).reshape(160, 128)
    force = pl.pallas_call(
        force_kernel,
        name="force",
        out_shape=jax.ShapeDtypeStruct((3, TILES, 128), jnp.float32),
        in_specs=[SMEM] * 4 + [VMEM] * 7,
        out_specs=VMEM,
        scratch_shapes=[pltpu.VMEM((ROWS, 128), jnp.float32)] * 3,
        compiler_params=PARAMS,
    )(base, count, first, widest, jf, tj, key, xi, yi, zi, ti)
    force = force.reshape(3, 2, 2, 8, 128)
    new_vel, heated = atom_update(
        force, velocities, kicks, live, subcell, electron_temp, laser_flux
    )
    temper = heated
    for substep in range(3):
        extended = with_halo(temper, (("gx", 0), ("gy", 1)), 1)
        temper = diffuse_padded(extended)
    return (new_vel, temper)


def solution(mesh):
    in_specs = (
        P(None, "gx", "gy", None, None),
        P(None, "gx", "gy", None, None),
        P(None, "gx", "gy", None, None),
        P("gx", "gy", None),
        P("gx", "gy", None, None),
        P("gx", "gy", None),
        P("gx", "gy"),
    )
    out_specs = (P(None, "gx", "gy", None, None), P("gx", "gy", None))
    return jax.shard_map(local, mesh=mesh, in_specs=in_specs, out_specs=out_specs, check_vma=False)
```

```python
import jax
import jax.numpy as jnp
import numpy as np
from jax import lax
from jax.experimental import pallas as pl
from jax.experimental.pallas import tpu as pltpu
from jax.sharding import PartitionSpec as P

ROOT = float(np.sqrt(5.0))
FAR = 1000.0 * ROOT
ROWS = 4096 + 64
TILES = 32
RANK_KEY = 1024
FAST = 3
f32 = jnp.float32
SIDES = [(dx, dy) for dx in (-1, 0, 1) for dy in (-1, 0, 1) if (dx, dy) != (0, 0)]


def static_tables():
    vertex = []
    for n in range(256):
        col, o, z = n // 64, n // 8 % 8, n % 8
        ox, oy, oz = o // 4, o // 2 % 2, o % 2
        vertex.append(((col // 2 + ox) * 3 + (col % 2 + oy)) * 9 + z + oz)
    vertex = np.array(vertex)
    order = np.argsort(vertex, kind="stable")
    rank = np.zeros(256, np.int64)
    rank[order] = np.arange(256)
    before = (rank[:, None] < rank[None, :]).astype(np.float32)
    start = (vertex[:, None] < np.arange(128)[None, :]).astype(np.float32)
    return order.astype(np.int32), before, start


def span(d, sender):
    if d == 0:
        return slice(0, 2) if sender else slice(1, 3)
    if sender:
        return slice(1, 2) if d > 0 else slice(0, 1)
    return slice(0, 1) if d > 0 else slice(3, 4)


def neighbour(dx, dy):
    nx, ny = lax.axis_size("gx"), lax.axis_size("gy")
    return (
        lax.rem(lax.axis_index("gx") + dx + nx, nx),
        lax.rem(lax.axis_index("gy") + dy + ny, ny),
    )


def greet():
    barrier = pltpu.get_barrier_semaphore()
    for dx, dy in SIDES:
        pl.semaphore_signal(
            barrier, inc=1, device_id=neighbour(dx, dy), device_id_type=pl.DeviceIdType.MESH
        )
    pl.semaphore_wait(barrier, len(SIDES))


def remote(src, dst, send, recv, dx, dy):
    return pltpu.make_async_remote_copy(
        src_ref=src,
        dst_ref=dst,
        send_sem=send,
        recv_sem=recv,
        device_id=neighbour(dx, dy),
        device_id_type=pl.DeviceIdType.MESH,
    )


def iota(shape, dim):
    return lax.broadcasted_iota(jnp.int32, shape, dim)


def wide(column):
    return jnp.broadcast_to(column, (8, 128))


def gather_kernel(
    pos, vel, kick, cnt, sub, te, flux, upper, before, start,
    jf, key, tab, heat, pv, halo, cbuf, hot, ssem, rsem, csem, dsem,
):
    greet()
    copies = []
    for n, (dx, dy) in enumerate(SIDES):
        copies.append(
            remote(
                pos.at[:, span(dx, True), span(dy, True)],
                halo.at[:, span(dx, False), span(dy, False)],
                ssem.at[n], rsem.at[n], dx, dy,
            )
        )
        copies.append(remote(cnt, cbuf.at[n], csem.at[n], dsem.at[n], dx, dy))
    for c in copies:
        c.start()

    lane, row = iota((8, 128), 1), iota((8, 128), 0)
    pick = iota((8, 8), 0) == iota((8, 8), 1)
    deep = row.astype(f32) - 4.0

    def alive(counts):
        column = jnp.sum(jnp.where(pick, counts.astype(f32), 0.0), axis=1, keepdims=True)
        return lane < wide(column).astype(jnp.int32)

    def features(hx, hy, xyz, live):
        at = (hx * 4 + hy) * 10 + 1
        out = []
        for n, off in enumerate((float(hx - 2), float(hy - 2), deep)):
            out.append(jnp.where(live, (xyz[n] + off) * ROOT, FAR))
            jf[n, at : at + 8, :] = out[n]
        jf[3, at : at + 8, :] = -(out[0] * out[0] + out[1] * out[1] + out[2] * out[2])

    for col in range(16):
        for z in (0, 9):
            for n in range(4):
                jf[n, col * 10 + z : col * 10 + z + 1, :] = jnp.full((1, 128), FAR if n < 3 else -3.0 * FAR * FAR, f32)

    for col in range(4):
        tx, ty = col // 2, col % 2
        live = alive(cnt[tx, pl.ds(ty, 8, stride=0), :])
        xyz = [pos[n, tx, ty] for n in range(3)]
        features(tx + 1, ty + 1, xyz, live)
        octant = sum(
            jnp.where(xyz[n] >= 0.5, s, 0) for n, s in enumerate((4, 2, 1))
        )
        octant = jnp.where(live, octant, -1)
        for o in range(8):
            hot[col * 64 + o * 8 : col * 64 + o * 8 + 8, :] = jnp.where(octant == o, 1.0, 0.0)
        upto = jnp.dot(
            hot[col * 64 : col * 64 + 64, :].astype(jnp.bfloat16), upper[...],
            preferred_element_type=f32,
        )
        rank = jnp.zeros((8, 128), f32)
        for o in range(8):
            rank = rank + jnp.where(octant == o, upto[o * 8 : o * 8 + 8, :], 0.0)
        key[col * 8 : col * 8 + 8, :] = jnp.where(
            live, octant * RANK_KEY + rank.astype(jnp.int32) - 1, -1
        )

        cell = jnp.where(live, sub[tx, ty], -1)
        te_atom = jnp.zeros((8, 128), f32)
        for a in range(3):
            for b in range(3):
                line = te[tx * 3 + a, pl.ds(ty * 3 + b, 8, stride=0), :]
                for c in range(3):
                    third = iota((8, 24), 1) == 3 * iota((8, 24), 0) + c
                    value = jnp.sum(jnp.where(third, line, 0.0), axis=1, keepdims=True)
                    te_atom = jnp.where(cell == 9 * a + 3 * b + c, wide(value), te_atom)
        sigma = jnp.sqrt(0.2 * te_atom)
        v = [vel[n, tx, ty] for n in range(3)]
        k = [kick[n, tx, ty] for n in range(3)]
        for n in range(3):
            pv[n, col * 8 : col * 8 + 8, :] = jnp.where(live, 0.9 * v[n] + sigma * k[n], 0.0)
        work = 0.1 * (v[0] * v[0] + v[1] * v[1] + v[2] * v[2]) - sigma * (
            k[0] * v[0] + k[1] * v[1] + k[2] * v[2]
        )
        depth = jnp.exp((iota((1, 128), 1).astype(f32) + 0.5) * (-1.0 / 38.0)) * 0.05
        for a in range(3):
            for b in range(3):
                grid = jnp.zeros((8, 128), f32)
                for c in range(3):
                    part = jnp.where(cell == 9 * a + 3 * b + c, work, 0.0)
                    value = wide(jnp.sum(part, axis=1, keepdims=True))
                    grid = jnp.where(lane == 3 * row + c, value, grid)
                gained = jnp.sum(grid, axis=0, keepdims=True)
                base = te[tx * 3 + a, ty * 3 + b : ty * 3 + b + 1, :]
                light = flux[tx * 3 + a, ty * 3 + b] * depth
                heat[tx, ty, a, b : b + 1, :] = gained * (1.0 / 40.0) + light
                heat[tx, ty, a, b : b + 1, 0:24] = heat[tx, ty, a, b : b + 1, 0:24] + base
        for a in range(3):
            heat[tx, ty, a, 3:8, :] = jnp.zeros((5, 128), f32)

    ones = jnp.ones((8, 128), jnp.bfloat16)
    count = lax.dot_general(
        ones, hot[...].astype(jnp.bfloat16), (((1,), (1,)), ((), ())), preferred_element_type=f32
    )
    few = count.astype(jnp.bfloat16)
    base = jnp.dot(few, before[...], preferred_element_type=f32)
    first = jnp.dot(few, start[...], preferred_element_type=f32)
    tab[0:1, :] = base[0:1, :].astype(jnp.int32)
    tab[1:2, :] = count[0:1, :].astype(jnp.int32)
    tab[2:3, 0:128] = first[0:1, :].astype(jnp.int32)
    tab[2:3, 128:256] = jnp.zeros((1, 128), jnp.int32)
    tab[3:8, :] = jnp.zeros((5, 256), jnp.int32)

    for c in copies:
        c.wait()
    for n, (dx, dy) in enumerate(SIDES):
        for hx in range(4)[span(dx, False)]:
            for hy in range(4)[span(dy, False)]:
                sx = hx - 1 if dx == 0 else (1 if dx > 0 else 0)
                sy = hy - 1 if dy == 0 else (1 if dy > 0 else 0)
                live = alive(cbuf[n, sx, pl.ds(sy, 8, stride=0), :])
                features(hx, hy, [halo[m, hx, hy] for m in range(3)], live)


def exchange_kernel(t, heat, t_all, heat_all, tbuf, hbuf, ssem, rsem, csem, dsem):
    greet()
    copies = []
    for n, (dx, dy) in enumerate(SIDES):
        sx, sy, rx, ry = span(dx, True), span(dy, True), span(dx, False), span(dy, False)
        copies.append(remote(t.at[sx, sy], tbuf.at[rx, ry], ssem.at[n], rsem.at[n], dx, dy))
        copies.append(remote(heat.at[sx, sy], hbuf.at[rx, ry], csem.at[n], dsem.at[n], dx, dy))
    for c in copies:
        c.start()
    t_all[...] = jnp.zeros_like(t_all)
    for x in range(2):
        for y in range(2):
            at = ((x + 1) * 4 + y + 1) * 10 + 1
            t_all[at : at + 8, :] = t[x, y]
            heat_all[x + 1, y + 1] = heat[x, y]
    for c in copies:
        c.wait()
    for x in range(4):
        for y in range(4):
            if x in (1, 2) and y in (1, 2):
                continue
            at = (x * 4 + y) * 10 + 1
            t_all[at : at + 8, :] = tbuf[x, y]
            heat_all[x, y] = hbuf[x, y]


def parts_of(item):
    return item // 64 * 8 + item % 8, item // 8 % 8


def own_tile(tile):
    return (tile // 16 + 1) * 40 + (tile // 8 % 2 + 1) * 10 + tile % 8 + 1


def over_items(tab, order, chunk):
    def step(i, carry):
        items = [order[i * 4 + u] for u in range(4)]
        widest = tab[1, items[0]]
        for item in items[1:]:
            widest = jnp.maximum(widest, tab[1, item])

        @pl.when(widest <= FAST * 8)
        def _():
            for item in items:
                for k in range(FAST):
                    chunk(item, *parts_of(item), k)

        @pl.when(widest > FAST * 8)
        def _():
            def one(u, carry):
                item = order[i * 4 + u]

                def inner(k, carry):
                    chunk(item, *parts_of(item), k)
                    return carry

                return lax.fori_loop(0, (tab[1, item] + 7) // 8, inner, carry)

            lax.fori_loop(0, 4, one, 0)

        return carry

    lax.fori_loop(0, 64, step, 0)


def over_tiles(tab, chunk, put, zero):
    def step(tile, carry):
        first = tile // 8 * 64 + tile % 8
        widest = tab[1, first]
        for o in range(1, 8):
            widest = jnp.maximum(widest, tab[1, first + o * 8])

        @pl.when(widest <= FAST * 8)
        def _():
            lanes = zero
            for o in range(8):
                for k in range(FAST):
                    lanes = chunk(first + o * 8, tile, o, k, lanes)
            put(tile, lanes)

        @pl.when(widest > FAST * 8)
        def _():
            def per(o, lanes):
                item = first + o * 8

                def inner(k, lanes):
                    return chunk(item, tile, o, k, lanes)

                return lax.fori_loop(0, (tab[1, item] + 7) // 8, inner, lanes)

            put(tile, lax.fori_loop(0, 8, per, zero))

        return carry

    lax.fori_loop(0, TILES, step, 0)


def over_vertices(tab, body):
    def column(c, carry):
        def level(z, carry):
            v = c * 9 + z
            first, last = tab[2, v], tab[2, v + 1]
            low = (c // 3) * 40 + (c % 3) * 10 + z

            def block(b, carry):
                body(first + b * 16, low)
                return carry

            return lax.fori_loop(0, (last - first + 15) // 16, block, carry)

        return lax.fori_loop(0, 9, level, carry)

    lax.fori_loop(0, 9, column, 0)


def around(low):
    return [low + dx * 40 + dy * 10 + dz for dx in (0, 1) for dy in (0, 1) for dz in (0, 1)]


def density_kernel(tab, order, jf, key, xi, yi, zi, ti, tl, acc):
    sub = iota((8, 128), 0)

    def match(tile, octant, k):
        return key[pl.ds(tile, 8, stride=0), :] == sub + (octant * RANK_KEY + k * 8)

    def expand(item, tile, octant, k):
        hit = match(tile, octant, k)
        row = tab[0, item] + k * 8
        at = own_tile(tile)
        for n, out in enumerate((xi, yi, zi)):
            value = jf[n, pl.ds(at, 8, stride=0), :]
            out[pl.ds(row, 8), :] = wide(jnp.sum(jnp.where(hit, value, 0.0), axis=1, keepdims=True))

    over_items(tab, order, expand)

    def body(row, low):
        x2, y2, z2, aa, tot = [], [], [], [], []
        for k in range(2):
            x, y, z = (r[pl.ds(row + 8 * k, 8), :] for r in (xi, yi, zi))
            aa.append(1.0 - (x * x + y * y + z * z))
            x2.append(x + x)
            y2.append(y + y)
            z2.append(z + z)
            tot.append(None)
        for tile in around(low):
            xj, yj, zj, bj = (jf[n, pl.ds(tile, 8, stride=0), :] for n in range(4))
            for k in range(2):
                w = (aa[k] + bj) + (x2[k] * xj + y2[k] * yj + z2[k] * zj)
                w = jnp.maximum(w, 0.0)
                cube = w * w * w
                tot[k] = cube if tot[k] is None else tot[k] + cube
        for k in range(2):
            acc[pl.ds(row + 8 * k, 8), :] = tot[k]

    over_vertices(tab, body)

    def rows(i, carry):
        for k in range(16):
            r = pl.multiple_of(i * 128, 128) + k * 8
            tot = jnp.sum(acc[pl.ds(r, 8), :], axis=1, keepdims=True)
            ti[pl.ds(r, 8), :] = wide(0.1875 + 0.625 * lax.rsqrt(tot))
        return carry

    lax.fori_loop(0, (tab[2, 81] + 127) // 128, rows, 0)

    def finish(item, tile, octant, k, lanes):
        t = ti[pl.ds(tab[0, item] + k * 8, 8), :]
        return lanes + jnp.where(match(tile, octant, k), t, 0.0)

    def put(tile, lanes):
        tl[pl.ds(tile, 1), :] = jnp.sum(lanes, axis=0, keepdims=True)

    over_tiles(tab, finish, put, jnp.zeros((8, 128), f32))


def diffuse(heat, out, old, new):
    for x in range(12):
        for y in range(4):
            old[x, y * 3 : y * 3 + 8, :] = heat[x // 3, y, x % 3]
    lane = iota((8, 128), 1)
    for s in range(3):
        for x in range(s + 1, 11 - s):
            for r in (1, 9) if s == 0 else (s + 1,):
                t = old[x, r : r + 8, :]
                near = [old[x - 1, r : r + 8, :], old[x + 1, r : r + 8, :], old[x, r - 1 : r + 7, :], old[x, r + 1 : r + 9, :]]
                q = t * t
                side = near[0] * near[0] + near[1] * near[1] + near[2] * near[2] + near[3] * near[3] - 4.0 * q
                up = jnp.where(lane < 23, pltpu.roll(q, 127, 1) - q, 0.0)
                t = t + 0.025 * (side + (up - pltpu.roll(up, 1, 1)))
                if s < 2:
                    new[x, r : r + 8, :] = t
                else:
                    out[x - 3, :, :] = t[0:6, 0:24]
        old, new = new, old


def force_kernel(tab, jf, tj, key, xi, yi, zi, ti, pv, heat, vel, temp, fx, fy, fz, old, new):
    sub = iota((8, 128), 0)

    def match(tile, octant, k):
        return key[pl.ds(tile, 8, stride=0), :] == sub + (octant * RANK_KEY + k * 8)

    diffuse(heat, temp, old, new)

    def body(row, low):
        own = [[r[pl.ds(row + 8 * k, 8), :] for r in (xi, yi, zi, ti)] for k in range(2)]
        tot = [[None] * 3, [None] * 3]
        for tile in around(low):
            other = [jf[n, pl.ds(tile, 8, stride=0), :] for n in range(3)]
            t_other = tj[pl.ds(tile, 8, stride=0), :]
            for k in range(2):
                d = [own[k][n] - other[n] for n in range(3)]
                w = jnp.maximum(1.0 - (d[0] * d[0] + d[1] * d[1] + d[2] * d[2]), 0.0)
                g = (w * w) * ((own[k][3] + t_other) - w)
                for n in range(3):
                    p = g * d[n]
                    tot[k][n] = p if tot[k][n] is None else tot[k][n] + p
        for k in range(2):
            for n, f in enumerate((fx, fy, fz)):
                f[pl.ds(row + 8 * k, 8), :] = tot[k][n]

    over_vertices(tab, body)

    def finish(item, tile, octant, k, lanes):
        row = tab[0, item] + k * 8
        hit = match(tile, octant, k)
        new_lanes = []
        for n, f in enumerate((fx, fy, fz)):
            tot = jnp.sum(f[pl.ds(row, 8), :], axis=1, keepdims=True)
            new_lanes.append(lanes[n] + jnp.where(hit, wide(tot), 0.0))
        return tuple(new_lanes)

    def put(tile, lanes):
        for n in range(3):
            total = jnp.sum(lanes[n], axis=0, keepdims=True)
            vel[n, pl.ds(tile, 1), :] = pv[n, pl.ds(tile, 1), :] + total * (-2.4 / ROOT)

    over_tiles(tab, finish, put, (jnp.zeros((8, 128), f32),) * 3)


VMEM = pl.BlockSpec(memory_space=pltpu.VMEM)
SMEM = pl.BlockSpec(memory_space=pltpu.SMEM)
LOCAL = pltpu.CompilerParams(vmem_limit_bytes=60 << 20)


def shape(*dims, dtype=f32):
    return jax.ShapeDtypeStruct(dims, dtype)


def meeting(n):
    return pltpu.CompilerParams(collective_id=n, has_side_effects=True, vmem_limit_bytes=32 << 20)


def local(positions, velocities, kicks, counts, subcell, electron_temp, laser_flux):
    order, before, start = static_tables()
    upper = np.triu(np.ones((128, 128), np.float32))
    bf = jnp.bfloat16
    dma = pltpu.SemaphoreType.DMA((8,))
    jf, key, tab, heat, pv = pl.pallas_call(
        gather_kernel,
        name="gather",
        out_shape=(
            shape(4, 160, 128),
            shape(TILES, 128, dtype=jnp.int32),
            shape(8, 256, dtype=jnp.int32),
            shape(2, 2, 3, 8, 128),
            shape(3, TILES, 128),
        ),
        in_specs=[VMEM] * 6 + [SMEM] + [VMEM] * 3,
        out_specs=(VMEM,) * 5,
        scratch_shapes=[
            pltpu.VMEM((3, 4, 4, 8, 128), f32),
            pltpu.VMEM((8, 2, 2, 8), jnp.int32),
            pltpu.VMEM((256, 128), f32),
            dma, dma, dma, dma,
        ],
        compiler_params=meeting(0),
    )(
        positions, velocities, kicks, counts, subcell, electron_temp, laser_flux,
        jnp.asarray(upper, bf), jnp.asarray(before, bf), jnp.asarray(start, bf),
    )
    order = jnp.asarray(order)
    row = shape(ROWS, 128)
    xi, yi, zi, ti, tl = pl.pallas_call(
        density_kernel,
        name="density",
        out_shape=(row, row, row, row, shape(TILES, 128)),
        in_specs=[SMEM] * 2 + [VMEM] * 2,
        out_specs=(VMEM,) * 5,
        scratch_shapes=[pltpu.VMEM((ROWS, 128), f32)],
        compiler_params=LOCAL,
    )(tab, order, jf, key)
    tj, heat = pl.pallas_call(
        exchange_kernel,
        name="exchange",
        out_shape=(shape(160, 128), shape(4, 4, 3, 8, 128)),
        in_specs=[VMEM] * 2,
        out_specs=(VMEM,) * 2,
        scratch_shapes=[
            pltpu.VMEM((4, 4, 8, 128), f32),
            pltpu.VMEM((4, 4, 3, 8, 128), f32),
            dma, dma, dma, dma,
        ],
        compiler_params=meeting(1),
    )(tl.reshape(2, 2, 8, 128), heat)
    vel, temp = pl.pallas_call(
        force_kernel,
        name="force",
        out_shape=(shape(3, TILES, 128), shape(6, 6, 24)),
        in_specs=[SMEM] + [VMEM] * 9,
        out_specs=(VMEM,) * 2,
        scratch_shapes=[pltpu.VMEM((ROWS, 128), f32)] * 3 + [pltpu.VMEM((12, 24, 128), f32)] * 2,
        compiler_params=LOCAL,
    )(tab, jf, tj, key, xi, yi, zi, ti, pv, heat)
    return (vel.reshape(3, 2, 2, 8, 128), temp)


def solution(mesh):
    in_specs = (
        P(None, "gx", "gy", None, None),
        P(None, "gx", "gy", None, None),
        P(None, "gx", "gy", None, None),
        P("gx", "gy", None),
        P("gx", "gy", None, None),
        P("gx", "gy", None),
        P("gx", "gy"),
    )
    out_specs = (P(None, "gx", "gy", None, None), P("gx", "gy", None))
    return jax.shard_map(local, mesh=mesh, in_specs=in_specs, out_specs=out_specs, check_vma=False)
```

```python
import jax
import jax.numpy as jnp
import numpy as np
from jax import lax
from jax.experimental import pallas as pl
from jax.experimental.pallas import tpu as pltpu
from jax.sharding import PartitionSpec as P

ROOT = float(np.sqrt(5.0))
FAR = 1000.0 * ROOT
ROWS = 4096 + 64
TILES = 32
RANK_KEY = 1024
FAST = 3
f32 = jnp.float32
SIDES = [(dx, dy) for dx in (-1, 0, 1) for dy in (-1, 0, 1) if (dx, dy) != (0, 0)]


COLUMN = 24
BLOCKS = 384
CHUNK = 32


def where_of(n):
    col, o, z = n // 64, n // 8 % 8, n % 8
    ox, oy, oz = o // 4, o // 2 % 2, o % 2
    return col, o, z, ((col // 2 + ox) * 3 + (col % 2 + oy)) * 9 + z + oz


def static_tables():
    col, o, z, vertex = (np.array(k) for k in zip(*(where_of(n) for n in range(256))))
    order = np.argsort(vertex, kind="stable")
    rank = np.zeros(256, np.int64)
    rank[order] = np.arange(256)
    before = rank[:, None] < rank[None, :]
    tile = col * 8 + z
    inside = (tile[:, None] == tile[None, :]) & (o[:, None] < o[None, :])
    at = vertex[:, None] == np.arange(128)[None, :]
    start = np.arange(128)[:, None] > vertex[None, :]
    return order.astype(np.int32), before, inside, at, start


def span(d, sender):
    if d == 0:
        return slice(0, 2) if sender else slice(1, 3)
    if sender:
        return slice(1, 2) if d > 0 else slice(0, 1)
    return slice(0, 1) if d > 0 else slice(3, 4)


def neighbour(dx, dy):
    nx, ny = lax.axis_size("gx"), lax.axis_size("gy")
    return (
        lax.rem(lax.axis_index("gx") + dx + nx, nx),
        lax.rem(lax.axis_index("gy") + dy + ny, ny),
    )


def greet():
    barrier = pltpu.get_barrier_semaphore()
    for dx, dy in SIDES:
        pl.semaphore_signal(
            barrier, inc=1, device_id=neighbour(dx, dy), device_id_type=pl.DeviceIdType.MESH
        )
    pl.semaphore_wait(barrier, len(SIDES))


def remote(src, dst, send, recv, dx, dy):
    return pltpu.make_async_remote_copy(
        src_ref=src,
        dst_ref=dst,
        send_sem=send,
        recv_sem=recv,
        device_id=neighbour(dx, dy),
        device_id_type=pl.DeviceIdType.MESH,
    )


def iota(shape, dim):
    return lax.broadcasted_iota(jnp.int32, shape, dim)


def wide(column):
    return jnp.broadcast_to(column, (8, 128))


def gather_kernel(
    pos_h, vel_h, kick_h, cnt_h, sub_h, te_h, flux_h, upper_h, before_h, inside_h, at_h, start_h,
    jf_h, key_h, tab_h, heat_h, pv_h, rows_h,
    pos, vel, kick, cnt, sub, te, flux, upper, before, inside, at, start,
    jf, key, tab, heat, pv, rows,
    halo, cbuf, hot, order, feat, insem, outsem, ssem, rsem, csem, dsem,
):
    loads = [
        pltpu.make_async_copy(src, dst, insem.at[n])
        for n, (src, dst) in enumerate(
            zip(
                (cnt_h, pos_h, upper_h, sub_h, te_h, vel_h, kick_h, flux_h, before_h, inside_h, at_h, start_h),
                (cnt, pos, upper, sub, te, vel, kick, flux, before, inside, at, start),
                strict=True,
            )
        )
    ]
    for c in loads:
        c.start()
    greet()
    copies = []
    for n, (dx, dy) in enumerate(SIDES):
        copies.append(
            remote(
                pos_h.at[:, span(dx, True), span(dy, True)],
                halo.at[:, span(dx, False), span(dy, False)],
                ssem.at[n], rsem.at[n], dx, dy,
            )
        )
        copies.append(remote(cnt_h, cbuf.at[n], csem.at[n], dsem.at[n], dx, dy))
    for c in copies:
        c.start()
    stores = [
        pltpu.make_async_copy(src, dst, outsem.at[n])
        for n, (src, dst) in enumerate(
            zip((rows, pv, heat, key, tab, jf), (rows_h, pv_h, heat_h, key_h, tab_h, jf_h), strict=True)
        )
    ]

    lane, row = iota((8, 128), 1), iota((8, 128), 0)
    pick = iota((8, 8), 0) == iota((8, 8), 1)
    deep = row.astype(f32) - 4.0

    def alive(counts):
        column = jnp.sum(jnp.where(pick, counts.astype(f32), 0.0), axis=1, keepdims=True)
        return lane < wide(column).astype(jnp.int32)

    def features(hx, hy, xyz, live):
        first = (hx * 4 + hy) * COLUMN + 8
        out = []
        for n, off in enumerate((float(hx - 2), float(hy - 2), deep)):
            out.append(jnp.where(live, (xyz[n] + off) * ROOT, FAR))
            jf[n, first : first + 8, :] = out[n]
        jf[3, first : first + 8, :] = -(out[0] * out[0] + out[1] * out[1] + out[2] * out[2])
        return out

    for col in range(16):
        for n in range(4):
            empty = jnp.full((8, 128), FAR if n < 3 else -3.0 * FAR * FAR, f32)
            jf[n, col * COLUMN : col * COLUMN + 8, :] = empty
            jf[n, col * COLUMN + 16 : col * COLUMN + 24, :] = empty

    for c in loads[:3]:
        c.wait()
    place = iota((128, 128), 0)
    ones = jnp.ones((128, 128), jnp.bfloat16)
    for n in range(9, 16):
        feat[:, n, :] = jnp.zeros((8, 128), f32)
    for col in range(4):
        tx, ty = col // 2, col % 2
        live = alive(cnt[tx, pl.ds(ty, 8, stride=0), :])
        xyz = [pos[n, tx, ty] for n in range(3)]
        own = features(tx + 1, ty + 1, xyz, live)
        octant = sum(
            jnp.where(xyz[n] >= 0.5, s, 0) for n, s in enumerate((4, 2, 1))
        )
        octant = jnp.where(live, octant, -1)
        for o in range(8):
            hot[col * 64 + o * 8 : col * 64 + o * 8 + 8, :] = jnp.where(octant == o, 1.0, 0.0)
        mine = hot[col * 64 : col * 64 + 64, :].astype(jnp.bfloat16)
        upto = jnp.dot(mine, upper[...], preferred_element_type=f32)
        total = jnp.dot(mine, ones, preferred_element_type=f32)
        rank = jnp.zeros((8, 128), f32)
        slot = jnp.zeros((8, 128), f32)
        ahead = jnp.zeros((8, 128), f32)
        for o in range(8):
            here = upto[o * 8 : o * 8 + 8, :]
            rank = jnp.where(octant == o, here, rank)
            slot = jnp.where(octant == o, here + ahead, slot)
            ahead = ahead + total[o * 8 : o * 8 + 8, :]
        key[col * 8 : col * 8 + 8, :] = jnp.where(
            live, octant * RANK_KEY + rank.astype(jnp.int32) - 1, -1
        )
        order[col * 8 : col * 8 + 8, :] = jnp.where(live, slot.astype(jnp.int32) - 1, -1)
        for n in range(3):
            high = own[n].astype(jnp.bfloat16).astype(f32)
            rest = own[n] - high
            middle = rest.astype(jnp.bfloat16).astype(f32)
            feat[:, n, :] = high
            feat[:, 3 + n, :] = middle
            feat[:, 6 + n, :] = rest - middle
        for z in range(8):
            tile = col * 8 + z
            hit = order[pl.ds(tile, 128, stride=0), :] == place
            rows[tile * 128 : tile * 128 + 128, 0:16] = lax.dot_general(
                jnp.where(hit, 1.0, 0.0).astype(jnp.bfloat16),
                feat[z].astype(jnp.bfloat16),
                (((1,), (1,)), ((), ())),
                preferred_element_type=f32,
            )
    stores[0].start()

    for c in loads[3:8]:
        c.wait()
    for col in range(4):
        tx, ty = col // 2, col % 2
        live = alive(cnt[tx, pl.ds(ty, 8, stride=0), :])
        cell = jnp.where(live, sub[tx, ty], -1)
        te_atom = jnp.zeros((8, 128), f32)
        for a in range(3):
            for b in range(3):
                line = te[tx * 3 + a, pl.ds(ty * 3 + b, 8, stride=0), :]
                for c in range(3):
                    third = iota((8, 24), 1) == 3 * iota((8, 24), 0) + c
                    value = jnp.sum(jnp.where(third, line, 0.0), axis=1, keepdims=True)
                    te_atom = jnp.where(cell == 9 * a + 3 * b + c, wide(value), te_atom)
        sigma = jnp.sqrt(0.2 * te_atom)
        v = [vel[n, tx, ty] for n in range(3)]
        k = [kick[n, tx, ty] for n in range(3)]
        for n in range(3):
            pv[n, col * 8 : col * 8 + 8, :] = jnp.where(live, 0.9 * v[n] + sigma * k[n], 0.0)
        work = 0.1 * (v[0] * v[0] + v[1] * v[1] + v[2] * v[2]) - sigma * (
            k[0] * v[0] + k[1] * v[1] + k[2] * v[2]
        )
        depth = jnp.exp((iota((1, 128), 1).astype(f32) + 0.5) * (-1.0 / 38.0)) * 0.05
        for a in range(3):
            for b in range(3):
                grid = jnp.zeros((8, 128), f32)
                for c in range(3):
                    part = jnp.where(cell == 9 * a + 3 * b + c, work, 0.0)
                    value = wide(jnp.sum(part, axis=1, keepdims=True))
                    grid = jnp.where(lane == 3 * row + c, value, grid)
                gained = jnp.sum(grid, axis=0, keepdims=True)
                base = te[tx * 3 + a, ty * 3 + b : ty * 3 + b + 1, :]
                light = flux[tx * 3 + a, ty * 3 + b] * depth
                heat[tx, ty, a, b : b + 1, :] = gained * (1.0 / 40.0) + light
                heat[tx, ty, a, b : b + 1, 0:24] = heat[tx, ty, a, b : b + 1, 0:24] + base
        for a in range(3):
            heat[tx, ty, a, 3:8, :] = jnp.zeros((5, 128), f32)
    for c in stores[1:4]:
        c.start()

    for c in loads[8:]:
        c.wait()
    bf = jnp.bfloat16
    both = (((1,), (1,)), ((), ()))
    count = lax.dot_general(ones[0:8], hot[...].astype(bf), both, preferred_element_type=f32)
    few = count.astype(bf)
    base = jnp.dot(few, before[...], preferred_element_type=f32)
    skip = jnp.dot(few, inside[...], preferred_element_type=f32)
    item = iota((1, 256), 1)
    tile = lax.shift_right_logical(item, 6) * 8 + (item & 7)
    tab[...] = jnp.zeros((8, BLOCKS), jnp.int32)
    tab[0:1, 0:256] = base[0:1, :].astype(jnp.int32)
    tab[1:2, 0:256] = skip[0:1, :].astype(jnp.int32) + tile * 128
    tab[2:3, 0:256] = count[0:1, :].astype(jnp.int32)
    many = jnp.dot(few, at[...], preferred_element_type=f32)
    blocks = lax.shift_right_logical(many.astype(jnp.int32) + 15, 4).astype(f32)
    rep = jnp.broadcast_to(blocks[0:1, :], (128, 128)).astype(bf)
    under = jnp.where(iota((128, 128), 1) < place, 1.0, 0.0).astype(bf)
    upon = jnp.where(iota((128, 128), 1) <= place, 1.0, 0.0).astype(bf)
    low_block = lax.dot_general(under, rep, both, preferred_element_type=f32)
    top_block = lax.dot_general(upon, rep, both, preferred_element_type=f32)
    first = lax.dot_general(
        start[...], jnp.broadcast_to(few[0:1, :].astype(f32), (128, 256)).astype(bf), both, preferred_element_type=f32
    )
    for j in range(BLOCKS // 128):
        b = (lane + 128 * j).astype(f32)
        begin = jnp.zeros((8, 128), f32)
        low = jnp.zeros((8, 128), f32)
        for r in range(11):
            base_tile = jnp.zeros((8, 128), f32)
            for s in range(8):
                v = r * 8 + s
                if v < 81:
                    c = v // 9
                    base_tile = jnp.where(
                        row == s, float(((c // 3) * 4 + c % 3) * COLUMN + 7 + v % 9), base_tile
                    )
            lo = low_block[r * 8 : r * 8 + 8, :]
            hit = (lo <= b) & (b < top_block[r * 8 : r * 8 + 8, :])
            begin = begin + jnp.where(hit, first[r * 8 : r * 8 + 8, :] + 16.0 * (b - lo), 0.0)
            low = low + jnp.where(hit, base_tile, 0.0)
        tab[3:4, j * 128 : j * 128 + 128] = jnp.sum(begin, axis=0, keepdims=True).astype(jnp.int32)
        tab[4:5, j * 128 : j * 128 + 128] = jnp.sum(low, axis=0, keepdims=True).astype(jnp.int32)
    tab[5:6, 0:128] = top_block[127:128, :].astype(jnp.int32)
    stores[4].start()

    for c in copies:
        c.wait()
    for n, (dx, dy) in enumerate(SIDES):
        for hx in range(4)[span(dx, False)]:
            for hy in range(4)[span(dy, False)]:
                sx = hx - 1 if dx == 0 else (1 if dx > 0 else 0)
                sy = hy - 1 if dy == 0 else (1 if dy > 0 else 0)
                live = alive(cbuf[n, sx, pl.ds(sy, 8, stride=0), :])
                features(hx, hy, [halo[m, hx, hy] for m in range(3)], live)
    stores[5].start()
    for c in stores:
        c.wait()


def exchange_kernel(t, heat, t_all, heat_all, own, ssem, rsem, csem, dsem):
    mine = [
        pltpu.make_async_copy(t, t_all.at[1:3, 1:3], own.at[0]),
        pltpu.make_async_copy(heat, heat_all.at[1:3, 1:3], own.at[1]),
    ]
    for c in mine:
        c.start()
    greet()
    copies = []
    for n, (dx, dy) in enumerate(SIDES):
        sx, sy, rx, ry = span(dx, True), span(dy, True), span(dx, False), span(dy, False)
        copies.append(remote(t.at[sx, sy], t_all.at[rx, ry], ssem.at[n], rsem.at[n], dx, dy))
        copies.append(remote(heat.at[sx, sy], heat_all.at[rx, ry], csem.at[n], dsem.at[n], dx, dy))
    for c in copies:
        c.start()
    for c in mine + copies:
        c.wait()


def own_tile(tile):
    return (tile // 16 + 1) * (4 * COLUMN) + (tile // 8 % 2 + 1) * COLUMN + tile % 8 + 8


def pack_rows(tab, order, rows, packed):
    def step(i, carry):
        items = [order[i * 8 + u] for u in range(8)]
        widest = tab[2, items[0]]
        for item in items[1:]:
            widest = jnp.maximum(widest, tab[2, item])

        @pl.when(widest <= FAST * 8)
        def _():
            for item in items:
                src, dst = tab[1, item], tab[0, item]
                for k in range(FAST):
                    packed[pl.ds(dst + 8 * k, 8), :] = rows[pl.ds(src + 8 * k, 8), :]

        @pl.when(widest > FAST * 8)
        def _():
            def one(u, carry):
                item = order[i * 8 + u]
                src, dst = tab[1, item], tab[0, item]

                def inner(k, carry):
                    packed[pl.ds(dst + 8 * k, 8), :] = rows[pl.ds(src + 8 * k, 8), :]
                    return carry

                return lax.fori_loop(0, (tab[2, item] + 7) // 8, inner, carry)

            lax.fori_loop(0, 8, one, 0)

        return carry

    lax.fori_loop(0, 32, step, 0)


def over_tiles(tab, chunk, put, zero):
    def step(tile, carry):
        first = tile // 8 * 64 + tile % 8
        widest = tab[2, first]
        for o in range(1, 8):
            widest = jnp.maximum(widest, tab[2, first + o * 8])

        @pl.when(widest <= FAST * 8)
        def _():
            lanes = zero
            for o in range(8):
                for k in range(FAST):
                    lanes = chunk(first + o * 8, tile, o, k, lanes)
            put(tile, lanes)

        @pl.when(widest > FAST * 8)
        def _():
            def per(o, lanes):
                item = first + o * 8

                def inner(k, lanes):
                    return chunk(item, tile, o, k, lanes)

                return lax.fori_loop(0, (tab[2, item] + 7) // 8, inner, lanes)

            put(tile, lax.fori_loop(0, 8, per, zero))

        return carry

    lax.fori_loop(0, TILES, step, 0)


def around(low):
    return [low + (dx * 4 + dy) * COLUMN + dz for dx in (0, 1) for dy in (0, 1) for dz in (0, 1)]


def matcher(key):
    sub = iota((8, 128), 0)

    def match(tile, octant, k):
        return key[pl.ds(tile, 8, stride=0), :] == sub + (octant * RANK_KEY + k * 8)

    return match


def slope_of(tot):
    return wide(0.1875 + 0.625 * lax.rsqrt(jnp.sum(tot, axis=1, keepdims=True)))


def density_kernel(
    tab_h, order_h, jf_h, key_h, rows_h, w_h, ti_h, tl_h,
    tab, order, jf, key, rows, packed, ti, tl, wb, insem, outsem, wsem,
):
    loads = [
        pltpu.make_async_copy(src, dst, insem.at[n])
        for n, (src, dst) in enumerate(((tab_h, tab), (order_h, order), (rows_h, rows.at[0:4096]), (jf_h, jf), (key_h, key)))
    ]
    for c in loads:
        c.start()
    for c in loads[:3]:
        c.wait()
    pack_rows(tab, order, rows, packed)
    for c in loads[3:]:
        c.wait()
    count = tab[5, 0]
    third = lax.rem(iota((8, 128), 1), 3)
    masks = [(third == n) & (iota((8, 128), 1) < 9) for n in range(3)]

    def own_rows(b):
        row = tab[3, b]
        out = []
        for k in range(2):
            value = packed[pl.ds(row + 8 * k, 8), :]
            x, y, z = (wide(jnp.sum(jnp.where(m, value, 0.0), axis=1, keepdims=True)) for m in masks)
            out += [x + x, y + y, z + z, 1.0 - (x * x + y * y + z * z)]
        return out

    def block(b, carry):
        own, last = carry[:8], carry[8:]
        ahead = own_rows(jnp.minimum(b + 1, BLOCKS - 1))
        tot = [None, None]
        for n, tile in enumerate(around(tab[4, b])):
            xj, yj, zj, bj = (jf[m, pl.ds(tile, 8, stride=0), :] for m in range(4))
            for k in range(2):
                x, y, z, a = own[4 * k : 4 * k + 4]
                w = jnp.maximum((a + bj) + (x * xj + y * yj + z * zj), 0.0)
                wb[b, (n * 2 + k) * 8 : (n * 2 + k) * 8 + 8, :] = w
                cube = w * w * w
                tot[k] = cube if tot[k] is None else tot[k] + cube
        row = tab[3, jnp.maximum(b - 1, 0)]
        for k in range(2):
            ti[pl.ds(row + 8 * k, 8), :] = slope_of(last[k])
        return (*ahead, *tot)

    def saved(g):
        part = pl.ds(g * CHUNK, CHUNK)
        return pltpu.make_async_copy(wb.at[part], w_h.at[part], wsem.at[g])

    def group(g, carry):
        carry = lax.fori_loop(g * CHUNK, jnp.minimum(g * CHUNK + CHUNK, count), block, carry)
        saved(g).start()
        return carry

    groups = (count + CHUNK - 1) // CHUNK
    one = jnp.ones((8, 128), f32)
    carry = lax.fori_loop(0, groups, group, (*own_rows(0), one, one))
    for k in range(2):
        ti[pl.ds(tab[3, count - 1] + 8 * k, 8), :] = slope_of(carry[8 + k])
    rows_out = pltpu.make_async_copy(ti, ti_h, outsem.at[0])
    rows_out.start()

    match = matcher(key)

    def finish(item, tile, octant, k, lanes):
        t = ti[pl.ds(tab[0, item] + k * 8, 8), :]
        return lanes + jnp.where(match(tile, octant, k), t, 0.0)

    def put(tile, lanes):
        tl[pl.ds(tile, 1), :] = jnp.sum(lanes, axis=0, keepdims=True)

    over_tiles(tab, finish, put, jnp.zeros((8, 128), f32))
    lanes_out = pltpu.make_async_copy(tl, tl_h, outsem.at[1])
    lanes_out.start()

    def drain(g, carry):
        saved(g).wait()
        return carry

    lax.fori_loop(0, groups, drain, 0)
    rows_out.wait()
    lanes_out.wait()


def diffuse(heat, out, old, new):
    for x in range(12):
        for y in range(4):
            old[x, y * 3 : y * 3 + 8, :] = heat[x // 3, y, x % 3]
    lane = iota((8, 128), 1)
    for s in range(3):
        for x in range(s + 1, 11 - s):
            for r in (1, 9) if s == 0 else (s + 1,):
                t = old[x, r : r + 8, :]
                near = [old[x - 1, r : r + 8, :], old[x + 1, r : r + 8, :], old[x, r - 1 : r + 7, :], old[x, r + 1 : r + 9, :]]
                q = t * t
                side = near[0] * near[0] + near[1] * near[1] + near[2] * near[2] + near[3] * near[3] - 4.0 * q
                up = jnp.where(lane < 23, pltpu.roll(q, 127, 1) - q, 0.0)
                t = t + 0.025 * (side + (up - pltpu.roll(up, 1, 1)))
                if s < 2:
                    new[x, r : r + 8, :] = t
                else:
                    out[x - 3, :, :] = t[0:6, 0:24]
        old, new = new, old


def force_kernel(
    tab_h, w_h, jf_h, tj_h, key_h, ti_h, pv_h, heat_h, vel_h, temp,
    tab, wb, jf, tj, key, ti, pv, heat, vel, fg, fx, fy, fz, old, new, insem, outsem, wsem,
):
    def loaded(g):
        part = pl.ds(g * CHUNK, CHUNK)
        return pltpu.make_async_copy(w_h.at[part], wb.at[part], wsem.at[g])

    loads = [
        pltpu.make_async_copy(src, dst, insem.at[n])
        for n, (src, dst) in enumerate(
            (
                (tab_h, tab), (heat_h, heat), (tj_h, tj.at[:, 8:16]), (ti_h, ti),
                (jf_h.at[0:3], jf), (key_h, key), (pv_h, pv),
            )
        )
    ]
    loads[0].start()
    loaded(0).start()
    for c in loads[1:]:
        c.start()
    loads[0].wait()
    count = tab[5, 0]
    groups = (count + CHUNK - 1) // CHUNK

    def fetch(g, carry):
        loaded(g).start()
        return carry

    lax.fori_loop(1, groups, fetch, 0)
    none = jnp.zeros((8, 128), f32)
    for col in range(16):
        tj[col, 0:8, :] = none
        tj[col, 16:24, :] = none
    loads[1].wait()
    diffuse(heat, temp, old, new)
    for c in loads[2:]:
        c.wait()
    sums = (fg, fx, fy, fz)

    def settle(row, last):
        for k in range(2):
            for n, f in enumerate(sums):
                f[pl.ds(row + 8 * k, 8), :] = wide(jnp.sum(last[4 * k + n], axis=1, keepdims=True))

    def block(b, last):
        low = tab[4, b]
        row = tab[3, b]
        t_own = [ti[pl.ds(row + 8 * k, 8), :] for k in range(2)]
        tot = [None] * 8
        for n in range(8):
            dx, dy, dz = n // 4, n // 2 % 2, n % 2
            tile = low + (dx * 4 + dy) * COLUMN + dz
            other = [jf[m, pl.ds(tile, 8, stride=0), :] for m in range(3)]
            t_other = tj.at[...].reshape(16 * COLUMN, 128)[pl.ds(tile, 8, stride=0), :]
            for k in range(2):
                w = wb[b, (n * 2 + k) * 8 : (n * 2 + k) * 8 + 8, :]
                g = (w * w) * ((t_own[k] + t_other) - w)
                for m, p in enumerate((g, g * other[0], g * other[1], g * other[2])):
                    at = 4 * k + m
                    tot[at] = p if tot[at] is None else tot[at] + p
        settle(tab[3, jnp.maximum(b - 1, 0)], last)
        return tuple(tot)

    def group(g, carry):
        loaded(g).wait()
        return lax.fori_loop(g * CHUNK, jnp.minimum(g * CHUNK + CHUNK, count), block, carry)

    settle(tab[3, count - 1], lax.fori_loop(0, groups, group, (none,) * 8))

    match = matcher(key)

    def finish(item, tile, octant, k, lanes):
        row = tab[0, item] + k * 8
        hit = match(tile, octant, k)
        return tuple(
            part + jnp.where(hit, f[pl.ds(row, 8), :], 0.0)
            for part, f in zip(lanes, sums, strict=True)
        )

    def put(tile, lanes):
        total = [jnp.sum(part, axis=0, keepdims=True) for part in lanes]
        at = own_tile(tile)
        live = key[pl.ds(tile, 1), :] >= 0
        for n in range(3):
            pull = jf[n, pl.ds(at, 1), :] * total[0] - total[n + 1]
            vel[n, pl.ds(tile, 1), :] = jnp.where(live, pv[n, pl.ds(tile, 1), :] + pull * (-2.4 / ROOT), 0.0)

    over_tiles(tab, finish, put, (none,) * 4)
    out = pltpu.make_async_copy(vel, vel_h, outsem.at[0])
    out.start()
    out.wait()


VMEM = pl.BlockSpec(memory_space=pltpu.VMEM)
ANY = pl.BlockSpec(memory_space=pl.ANY)
LOCAL = pltpu.CompilerParams(vmem_limit_bytes=60 << 20)


def shape(*dims, dtype=f32):
    return jax.ShapeDtypeStruct(dims, dtype)


def vmem(like):
    return pltpu.VMEM(like.shape, like.dtype)


def meeting(n):
    return pltpu.CompilerParams(collective_id=n, has_side_effects=True, vmem_limit_bytes=32 << 20)


def local(positions, velocities, kicks, counts, subcell, electron_temp, laser_flux):
    order, *zeroone = static_tables()
    upper = np.triu(np.ones((128, 128)))
    bf = jnp.bfloat16
    i32 = jnp.int32
    dma = pltpu.SemaphoreType.DMA
    around8 = [dma((8,))] * 4
    tiles = shape(3, 2, 2, 8, 128)
    outs = (
        shape(4, 16 * COLUMN, 128),
        shape(TILES, 128, dtype=i32),
        shape(8, BLOCKS, dtype=i32),
        shape(2, 2, 3, 8, 128),
        shape(3, TILES, 128),
        shape(4096, 128),
    )
    jf, key, tab, heat, pv, rows = pl.pallas_call(
        gather_kernel,
        name="gather",
        out_shape=outs,
        in_specs=[ANY] * 12,
        out_specs=(ANY,) * 6,
        scratch_shapes=[
            *(vmem(tiles),) * 3,
            pltpu.VMEM((2, 2, 8), i32),
            pltpu.VMEM((2, 2, 8, 128), i32),
            pltpu.VMEM((6, 6, 24), f32),
            pltpu.SMEM((6, 6), f32),
            pltpu.VMEM((128, 128), bf),
            *(pltpu.VMEM(m.shape, bf) for m in zeroone),
            *(vmem(o) for o in outs),
            pltpu.VMEM((3, 4, 4, 8, 128), f32),
            pltpu.VMEM((8, 2, 2, 8), i32),
            pltpu.VMEM((256, 128), f32),
            pltpu.VMEM((TILES, 128), i32),
            pltpu.VMEM((8, 16, 128), f32),
            dma((12,)),
            dma((6,)),
            *around8,
        ],
        compiler_params=meeting(0),
    )(
        positions, velocities, kicks, counts, subcell, electron_temp, laser_flux,
        *(jnp.asarray(m, bf) for m in (upper, *zeroone)),
    )
    order = jnp.asarray(order)
    row = shape(ROWS, 128)
    w, ti, tl = pl.pallas_call(
        density_kernel,
        name="density",
        out_shape=(shape(BLOCKS, 128, 128), row, shape(TILES, 128)),
        in_specs=[ANY] * 5,
        out_specs=(ANY,) * 3,
        scratch_shapes=[
            pltpu.SMEM((8, BLOCKS), i32),
            pltpu.SMEM((256,), i32),
            vmem(outs[0]),
            vmem(outs[1]),
            vmem(row),
            vmem(row),
            vmem(row),
            pltpu.VMEM((TILES, 128), f32),
            pltpu.VMEM((BLOCKS, 128, 128), f32),
            dma((5,)),
            dma((2,)),
            dma((BLOCKS // CHUNK,)),
        ],
        compiler_params=LOCAL,
    )(tab, order, jf, key, rows)
    t_all, heat = pl.pallas_call(
        exchange_kernel,
        name="exchange",
        out_shape=(shape(4, 4, 8, 128), shape(4, 4, 3, 8, 128)),
        in_specs=[ANY] * 2,
        out_specs=(ANY,) * 2,
        scratch_shapes=[dma((2,)), *around8],
        compiler_params=meeting(1),
    )(tl.reshape(2, 2, 8, 128), heat)
    vel, temp = pl.pallas_call(
        force_kernel,
        name="force",
        out_shape=(shape(3, TILES, 128), shape(6, 6, 24)),
        in_specs=[ANY] * 8,
        out_specs=(ANY, VMEM),
        scratch_shapes=[
            pltpu.SMEM((8, BLOCKS), i32),
            pltpu.VMEM((BLOCKS, 128, 128), f32),
            pltpu.VMEM((3, 16 * COLUMN, 128), f32),
            pltpu.VMEM((16, COLUMN, 128), f32),
            vmem(outs[1]),
            vmem(row),
            vmem(outs[4]),
            pltpu.VMEM((4, 4, 3, 8, 128), f32),
            vmem(outs[4]),
            *(vmem(row),) * 4,
            *(pltpu.VMEM((12, 24, 128), f32),) * 2,
            dma((7,)),
            dma((1,)),
            dma((BLOCKS // CHUNK,)),
        ],
        compiler_params=LOCAL,
    )(tab, w, jf, t_all.reshape(16, 8, 128), key, ti, pv, heat)
    return (vel.reshape(3, 2, 2, 8, 128), temp)


def solution(mesh):
    in_specs = (
        P(None, "gx", "gy", None, None),
        P(None, "gx", "gy", None, None),
        P(None, "gx", "gy", None, None),
        P("gx", "gy", None),
        P("gx", "gy", None, None),
        P("gx", "gy", None),
        P("gx", "gy"),
    )
    out_specs = (P(None, "gx", "gy", None, None), P("gx", "gy", None))
    return jax.shard_map(local, mesh=mesh, in_specs=in_specs, out_specs=out_specs, check_vma=False)
```

```python
import jax
import jax.numpy as jnp
import numpy as np
from jax import lax
from jax.experimental import pallas as pl
from jax.experimental.pallas import tpu as pltpu
from jax.sharding import PartitionSpec as P

ROOT = float(np.sqrt(5.0))
FAR = 1000.0 * ROOT
ROWS = 4096 + 64
TILES = 32
RANK_KEY = 1024
FAST = 3
f32 = jnp.float32
SIDES = [(dx, dy) for dx in (-1, 0, 1) for dy in (-1, 0, 1) if (dx, dy) != (0, 0)]


COLUMN = 24
BLOCKS = 384
CHUNK = 32
STEP = 4
SPARE = 4128


def where_of(n):
    col, o, z = n // 64, n // 8 % 8, n % 8
    ox, oy, oz = o // 4, o // 2 % 2, o % 2
    return col, o, z, ((col // 2 + ox) * 3 + (col % 2 + oy)) * 9 + z + oz


def static_tables():
    col, o, z, vertex = (np.array(k) for k in zip(*(where_of(n) for n in range(256))))
    order = np.argsort(vertex, kind="stable")
    rank = np.zeros(256, np.int64)
    rank[order] = np.arange(256)
    before = rank[:, None] < rank[None, :]
    tile = col * 8 + z
    inside = (tile[:, None] == tile[None, :]) & (o[:, None] < o[None, :])
    at = vertex[:, None] == np.arange(128)[None, :]
    start = np.arange(128)[:, None] > vertex[None, :]
    return order.astype(np.int32), before, inside, at, start


def span(d, sender):
    if d == 0:
        return slice(0, 2) if sender else slice(1, 3)
    if sender:
        return slice(1, 2) if d > 0 else slice(0, 1)
    return slice(0, 1) if d > 0 else slice(3, 4)


def neighbour(dx, dy):
    nx, ny = lax.axis_size("gx"), lax.axis_size("gy")
    return (
        lax.rem(lax.axis_index("gx") + dx + nx, nx),
        lax.rem(lax.axis_index("gy") + dy + ny, ny),
    )


def greet():
    barrier = pltpu.get_barrier_semaphore()
    for dx, dy in SIDES:
        pl.semaphore_signal(
            barrier, inc=1, device_id=neighbour(dx, dy), device_id_type=pl.DeviceIdType.MESH
        )
    pl.semaphore_wait(barrier, len(SIDES))


def remote(src, dst, send, recv, dx, dy):
    return pltpu.make_async_remote_copy(
        src_ref=src,
        dst_ref=dst,
        send_sem=send,
        recv_sem=recv,
        device_id=neighbour(dx, dy),
        device_id_type=pl.DeviceIdType.MESH,
    )


def iota(shape, dim):
    return lax.broadcasted_iota(jnp.int32, shape, dim)


def wide(column):
    return jnp.broadcast_to(column, (8, 128))


def gather_kernel(
    pos_h, vel_h, kick_h, cnt_h, sub_h, te_h, flux_h, upper_h, before_h, inside_h, at_h, start_h,
    jf_h, key_h, tab_h, heat_h, pv_h, rows_h,
    pos, vel, kick, cnt, sub, te, flux, upper, before, inside, at, start,
    jf, key, tab, heat, pv, rows,
    halo, cbuf, hot, order, feat, insem, outsem, ssem, rsem, csem, dsem,
):
    loads = [
        pltpu.make_async_copy(src, dst, insem.at[n])
        for n, (src, dst) in enumerate(
            zip(
                (cnt_h, pos_h, upper_h, sub_h, te_h, vel_h, kick_h, flux_h, before_h, inside_h, at_h, start_h),
                (cnt, pos, upper, sub, te, vel, kick, flux, before, inside, at, start),
                strict=True,
            )
        )
    ]
    for c in loads:
        c.start()
    greet()
    copies = []
    for n, (dx, dy) in enumerate(SIDES):
        copies.append(
            remote(
                pos_h.at[:, span(dx, True), span(dy, True)],
                halo.at[:, span(dx, False), span(dy, False)],
                ssem.at[n], rsem.at[n], dx, dy,
            )
        )
        copies.append(remote(cnt_h, cbuf.at[n], csem.at[n], dsem.at[n], dx, dy))
    for c in copies:
        c.start()
    stores = [
        pltpu.make_async_copy(src, dst, outsem.at[n])
        for n, (src, dst) in enumerate(
            zip((rows, pv, heat, key, tab, jf), (rows_h, pv_h, heat_h, key_h, tab_h, jf_h), strict=True)
        )
    ]

    lane, row = iota((8, 128), 1), iota((8, 128), 0)
    pick = iota((8, 8), 0) == iota((8, 8), 1)
    deep = row.astype(f32) - 4.0

    def alive(counts):
        column = jnp.sum(jnp.where(pick, counts.astype(f32), 0.0), axis=1, keepdims=True)
        return lane < wide(column).astype(jnp.int32)

    def features(hx, hy, xyz, live):
        first = (hx * 4 + hy) * COLUMN + 8
        out = []
        for n, off in enumerate((float(hx - 2), float(hy - 2), deep)):
            out.append(jnp.where(live, (xyz[n] + off) * ROOT, FAR))
            jf[n, first : first + 8, :] = out[n]
        jf[3, first : first + 8, :] = -(out[0] * out[0] + out[1] * out[1] + out[2] * out[2])
        return out

    for col in range(16):
        for n in range(4):
            empty = jnp.full((8, 128), FAR if n < 3 else -3.0 * FAR * FAR, f32)
            jf[n, col * COLUMN : col * COLUMN + 8, :] = empty
            jf[n, col * COLUMN + 16 : col * COLUMN + 24, :] = empty

    for c in loads[:3]:
        c.wait()
    place = iota((128, 128), 0)
    ones = jnp.ones((128, 128), jnp.bfloat16)
    for n in range(9, 16):
        feat[:, n, :] = jnp.zeros((8, 128), f32)
    for col in range(4):
        tx, ty = col // 2, col % 2
        live = alive(cnt[tx, pl.ds(ty, 8, stride=0), :])
        xyz = [pos[n, tx, ty] for n in range(3)]
        own = features(tx + 1, ty + 1, xyz, live)
        octant = sum(
            jnp.where(xyz[n] >= 0.5, s, 0) for n, s in enumerate((4, 2, 1))
        )
        octant = jnp.where(live, octant, -1)
        for o in range(8):
            hot[col * 64 + o * 8 : col * 64 + o * 8 + 8, :] = jnp.where(octant == o, 1.0, 0.0)
        mine = hot[col * 64 : col * 64 + 64, :].astype(jnp.bfloat16)
        upto = jnp.dot(mine, upper[...], preferred_element_type=f32)
        total = jnp.dot(mine, ones, preferred_element_type=f32)
        rank = jnp.zeros((8, 128), f32)
        slot = jnp.zeros((8, 128), f32)
        ahead = jnp.zeros((8, 128), f32)
        for o in range(8):
            here = upto[o * 8 : o * 8 + 8, :]
            rank = jnp.where(octant == o, here, rank)
            slot = jnp.where(octant == o, here + ahead, slot)
            ahead = ahead + total[o * 8 : o * 8 + 8, :]
        key[col * 8 : col * 8 + 8, :] = jnp.where(
            live, octant * RANK_KEY + rank.astype(jnp.int32) - 1, -1
        )
        order[col * 8 : col * 8 + 8, :] = jnp.where(live, slot.astype(jnp.int32) - 1, -1)
        for n in range(3):
            high = own[n].astype(jnp.bfloat16).astype(f32)
            rest = own[n] - high
            middle = rest.astype(jnp.bfloat16).astype(f32)
            feat[:, n, :] = high
            feat[:, 3 + n, :] = middle
            feat[:, 6 + n, :] = rest - middle
        for z in range(8):
            tile = col * 8 + z
            hit = order[pl.ds(tile, 128, stride=0), :] == place
            rows[tile * 128 : tile * 128 + 128, 0:16] = lax.dot_general(
                jnp.where(hit, 1.0, 0.0).astype(jnp.bfloat16),
                feat[z].astype(jnp.bfloat16),
                (((1,), (1,)), ((), ())),
                preferred_element_type=f32,
            )
    stores[0].start()

    for c in loads[3:8]:
        c.wait()
    for col in range(4):
        tx, ty = col // 2, col % 2
        live = alive(cnt[tx, pl.ds(ty, 8, stride=0), :])
        cell = jnp.where(live, sub[tx, ty], -1)
        te_atom = jnp.zeros((8, 128), f32)
        for a in range(3):
            for b in range(3):
                line = te[tx * 3 + a, pl.ds(ty * 3 + b, 8, stride=0), :]
                for c in range(3):
                    third = iota((8, 24), 1) == 3 * iota((8, 24), 0) + c
                    value = jnp.sum(jnp.where(third, line, 0.0), axis=1, keepdims=True)
                    te_atom = jnp.where(cell == 9 * a + 3 * b + c, wide(value), te_atom)
        sigma = jnp.sqrt(0.2 * te_atom)
        v = [vel[n, tx, ty] for n in range(3)]
        k = [kick[n, tx, ty] for n in range(3)]
        for n in range(3):
            pv[n, col * 8 : col * 8 + 8, :] = jnp.where(live, 0.9 * v[n] + sigma * k[n], 0.0)
        work = 0.1 * (v[0] * v[0] + v[1] * v[1] + v[2] * v[2]) - sigma * (
            k[0] * v[0] + k[1] * v[1] + k[2] * v[2]
        )
        depth = jnp.exp((iota((1, 128), 1).astype(f32) + 0.5) * (-1.0 / 38.0)) * 0.05
        for a in range(3):
            for b in range(3):
                grid = jnp.zeros((8, 128), f32)
                for c in range(3):
                    part = jnp.where(cell == 9 * a + 3 * b + c, work, 0.0)
                    value = wide(jnp.sum(part, axis=1, keepdims=True))
                    grid = jnp.where(lane == 3 * row + c, value, grid)
                gained = jnp.sum(grid, axis=0, keepdims=True)
                base = te[tx * 3 + a, ty * 3 + b : ty * 3 + b + 1, :]
                light = flux[tx * 3 + a, ty * 3 + b] * depth
                heat[tx, ty, a, b : b + 1, :] = gained * (1.0 / 40.0) + light
                heat[tx, ty, a, b : b + 1, 0:24] = heat[tx, ty, a, b : b + 1, 0:24] + base
        for a in range(3):
            heat[tx, ty, a, 3:8, :] = jnp.zeros((5, 128), f32)
    for c in stores[1:4]:
        c.start()

    for c in loads[8:]:
        c.wait()
    bf = jnp.bfloat16
    both = (((1,), (1,)), ((), ()))
    count = lax.dot_general(ones[0:8], hot[...].astype(bf), both, preferred_element_type=f32)
    few = count.astype(bf)
    base = jnp.dot(few, before[...], preferred_element_type=f32)
    skip = jnp.dot(few, inside[...], preferred_element_type=f32)
    item = iota((1, 256), 1)
    tile = lax.shift_right_logical(item, 6) * 8 + (item & 7)
    tab[...] = jnp.zeros((8, BLOCKS), jnp.int32)
    tab[0:1, 0:256] = base[0:1, :].astype(jnp.int32)
    tab[1:2, 0:256] = skip[0:1, :].astype(jnp.int32) + tile * 128
    tab[2:3, 0:256] = count[0:1, :].astype(jnp.int32)
    many = jnp.dot(few, at[...], preferred_element_type=f32)
    blocks = lax.shift_right_logical(many.astype(jnp.int32) + 15, 4).astype(f32)
    rep = jnp.broadcast_to(blocks[0:1, :], (128, 128)).astype(bf)
    under = jnp.where(iota((128, 128), 1) < place, 1.0, 0.0).astype(bf)
    upon = jnp.where(iota((128, 128), 1) <= place, 1.0, 0.0).astype(bf)
    low_block = lax.dot_general(under, rep, both, preferred_element_type=f32)
    top_block = lax.dot_general(upon, rep, both, preferred_element_type=f32)
    first = lax.dot_general(
        start[...], jnp.broadcast_to(few[0:1, :].astype(f32), (128, 256)).astype(bf), both, preferred_element_type=f32
    )
    for j in range(BLOCKS // 128):
        b = (lane + 128 * j).astype(f32)
        begin = jnp.zeros((8, 128), f32)
        low = jnp.zeros((8, 128), f32)
        for r in range(11):
            base_tile = jnp.zeros((8, 128), f32)
            for s in range(8):
                v = r * 8 + s
                if v < 81:
                    c = v // 9
                    base_tile = jnp.where(
                        row == s, float(((c // 3) * 4 + c % 3) * COLUMN + 7 + v % 9), base_tile
                    )
            lo = low_block[r * 8 : r * 8 + 8, :]
            hit = (lo <= b) & (b < top_block[r * 8 : r * 8 + 8, :])
            begin = begin + jnp.where(hit, first[r * 8 : r * 8 + 8, :] + 16.0 * (b - lo) - SPARE, 0.0)
            low = low + jnp.where(hit, base_tile, 0.0)
        tab[3:4, j * 128 : j * 128 + 128] = (jnp.sum(begin, axis=0, keepdims=True) + SPARE).astype(jnp.int32)
        tab[4:5, j * 128 : j * 128 + 128] = jnp.sum(low, axis=0, keepdims=True).astype(jnp.int32)
    tab[5:6, 0:128] = top_block[127:128, :].astype(jnp.int32)
    stores[4].start()

    for c in copies:
        c.wait()
    for n, (dx, dy) in enumerate(SIDES):
        for hx in range(4)[span(dx, False)]:
            for hy in range(4)[span(dy, False)]:
                sx = hx - 1 if dx == 0 else (1 if dx > 0 else 0)
                sy = hy - 1 if dy == 0 else (1 if dy > 0 else 0)
                live = alive(cbuf[n, sx, pl.ds(sy, 8, stride=0), :])
                features(hx, hy, [halo[m, hx, hy] for m in range(3)], live)
    stores[5].start()
    for c in stores:
        c.wait()


def exchange_kernel(t, heat, t_all, heat_all, own, ssem, rsem, csem, dsem):
    mine = [
        pltpu.make_async_copy(t, t_all.at[1:3, 1:3], own.at[0]),
        pltpu.make_async_copy(heat, heat_all.at[1:3, 1:3], own.at[1]),
    ]
    for c in mine:
        c.start()
    greet()
    copies = []
    for n, (dx, dy) in enumerate(SIDES):
        sx, sy, rx, ry = span(dx, True), span(dy, True), span(dx, False), span(dy, False)
        copies.append(remote(t.at[sx, sy], t_all.at[rx, ry], ssem.at[n], rsem.at[n], dx, dy))
        copies.append(remote(heat.at[sx, sy], heat_all.at[rx, ry], csem.at[n], dsem.at[n], dx, dy))
    for c in copies:
        c.start()
    for c in mine + copies:
        c.wait()


def own_tile(tile):
    return (tile // 16 + 1) * (4 * COLUMN) + (tile // 8 % 2 + 1) * COLUMN + tile % 8 + 8


def pack_rows(tab, order, rows, packed):
    def step(i, carry):
        items = [order[i * 8 + u] for u in range(8)]
        widest = tab[2, items[0]]
        for item in items[1:]:
            widest = jnp.maximum(widest, tab[2, item])

        @pl.when(widest <= FAST * 8)
        def _():
            for item in items:
                src, dst = tab[1, item], tab[0, item]
                for k in range(FAST):
                    packed[pl.ds(dst + 8 * k, 8), :] = rows[pl.ds(src + 8 * k, 8), :]

        @pl.when(widest > FAST * 8)
        def _():
            def one(u, carry):
                item = order[i * 8 + u]
                src, dst = tab[1, item], tab[0, item]

                def inner(k, carry):
                    packed[pl.ds(dst + 8 * k, 8), :] = rows[pl.ds(src + 8 * k, 8), :]
                    return carry

                return lax.fori_loop(0, (tab[2, item] + 7) // 8, inner, carry)

            lax.fori_loop(0, 8, one, 0)

        return carry

    lax.fori_loop(0, 32, step, 0)


def over_tiles(tab, chunk, put, zero):
    def step(tile, carry):
        first = tile // 8 * 64 + tile % 8
        widest = tab[2, first]
        for o in range(1, 8):
            widest = jnp.maximum(widest, tab[2, first + o * 8])

        @pl.when(widest <= FAST * 8)
        def _():
            lanes = zero
            for o in range(8):
                for k in range(FAST):
                    lanes = chunk(first + o * 8, tile, o, k, lanes)
            put(tile, lanes)

        @pl.when(widest > FAST * 8)
        def _():
            def per(o, lanes):
                item = first + o * 8

                def inner(k, lanes):
                    return chunk(item, tile, o, k, lanes)

                return lax.fori_loop(0, (tab[2, item] + 7) // 8, inner, lanes)

            put(tile, lax.fori_loop(0, 8, per, zero))

        return carry

    lax.fori_loop(0, TILES, step, 0)


def around(low):
    return [low + (dx * 4 + dy) * COLUMN + dz for dx in (0, 1) for dy in (0, 1) for dz in (0, 1)]


def matcher(key):
    sub = iota((8, 128), 0)

    def match(tile, octant, k):
        return key[pl.ds(tile, 8, stride=0), :] == sub + (octant * RANK_KEY + k * 8)

    return match


def slope_of(tot):
    return wide(0.1875 + 0.625 * lax.rsqrt(jnp.sum(tot, axis=1, keepdims=True)))


def density_kernel(
    tab_h, order_h, jf_h, key_h, rows_h, w_h, ti_h, tl_h,
    tab, order, jf, key, rows, packed, ti, tl, wb, own, last, insem, outsem, wsem,
):
    loads = [
        pltpu.make_async_copy(src, dst, insem.at[n])
        for n, (src, dst) in enumerate(((tab_h, tab), (order_h, order), (rows_h, rows.at[0:4096]), (jf_h, jf), (key_h, key)))
    ]
    for c in loads:
        c.start()
    for c in loads[:3]:
        c.wait()
    pack_rows(tab, order, rows, packed)
    for c in loads[3:]:
        c.wait()
    count = tab[5, 0]
    third = lax.rem(iota((8, 128), 1), 3)
    masks = [(third == n) & (iota((8, 128), 1) < 9) for n in range(3)]

    def own_rows(b):
        row = tab[3, b]
        out = []
        for k in range(2):
            value = packed[pl.ds(row + 8 * k, 8), :]
            x, y, z = (wide(jnp.sum(jnp.where(m, value, 0.0), axis=1, keepdims=True)) for m in masks)
            out += [x + x, y + y, z + z, 1.0 - (x * x + y * y + z * z)]
        return out

    def keep(blocks):
        for u, values in enumerate(blocks):
            for n, value in enumerate(values):
                own[u, n] = value

    def settle(i, tots):
        for u in range(STEP):
            row = tab[3, i * STEP + u]
            for k in range(2):
                ti[pl.ds(row + 8 * k, 8), :] = slope_of(tots[u][k])

    def step(i, carry):
        tots = [[last[u, k] for k in range(2)] for u in range(STEP)]
        ahead = [own_rows((i + 1) * STEP + u) for u in range(STEP)]
        new = []
        for u in range(STEP):
            b = i * STEP + u
            mine = [[own[u, 4 * k + n] for n in range(4)] for k in range(2)]
            tot = [None, None]
            for n, tile in enumerate(around(tab[4, b])):
                xj, yj, zj, bj = (jf[m, pl.ds(tile, 8, stride=0), :] for m in range(4))
                for k in range(2):
                    x, y, z, a = mine[k]
                    w = jnp.maximum((a + bj) + (x * xj + y * yj + z * zj), 0.0)
                    wb[b, (n * 2 + k) * 8 : (n * 2 + k) * 8 + 8, :] = w
                    cube = w * w * w
                    tot[k] = cube if tot[k] is None else tot[k] + cube
            new.append(tot)
        settle(jnp.maximum(i - 1, 0), tots)
        keep(ahead)
        for u in range(STEP):
            for k in range(2):
                last[u, k] = new[u][k]
        return carry

    def saved(g):
        part = pl.ds(g * CHUNK, CHUNK)
        return pltpu.make_async_copy(wb.at[part], w_h.at[part], wsem.at[g])

    steps = (count + STEP - 1) // STEP
    groups = (count + CHUNK - 1) // CHUNK
    per = CHUNK // STEP

    def group(g, carry):
        lax.fori_loop(g * per, jnp.minimum(g * per + per, steps), step, 0)
        saved(g).start()
        return carry

    keep([own_rows(u) for u in range(STEP)])
    last[...] = jnp.ones_like(last)
    lax.fori_loop(0, groups, group, 0)
    settle(steps - 1, [[last[u, k] for k in range(2)] for u in range(STEP)])
    rows_out = pltpu.make_async_copy(ti, ti_h, outsem.at[0])
    rows_out.start()

    match = matcher(key)

    def finish(item, tile, octant, k, lanes):
        t = ti[pl.ds(tab[0, item] + k * 8, 8), :]
        return lanes + jnp.where(match(tile, octant, k), t, 0.0)

    def put(tile, lanes):
        tl[pl.ds(tile, 1), :] = jnp.sum(lanes, axis=0, keepdims=True)

    over_tiles(tab, finish, put, jnp.zeros((8, 128), f32))
    lanes_out = pltpu.make_async_copy(tl, tl_h, outsem.at[1])
    lanes_out.start()

    def drain(g, carry):
        saved(g).wait()
        return carry

    lax.fori_loop(0, groups, drain, 0)
    rows_out.wait()
    lanes_out.wait()


def diffuse(heat, out, old, new):
    for x in range(12):
        for y in range(4):
            old[x, y * 3 : y * 3 + 8, :] = heat[x // 3, y, x % 3]
    lane = iota((8, 128), 1)
    for s in range(3):
        for x in range(s + 1, 11 - s):
            for r in (1, 9) if s == 0 else (s + 1,):
                t = old[x, r : r + 8, :]
                near = [old[x - 1, r : r + 8, :], old[x + 1, r : r + 8, :], old[x, r - 1 : r + 7, :], old[x, r + 1 : r + 9, :]]
                q = t * t
                side = near[0] * near[0] + near[1] * near[1] + near[2] * near[2] + near[3] * near[3] - 4.0 * q
                up = jnp.where(lane < 23, pltpu.roll(q, 127, 1) - q, 0.0)
                t = t + 0.025 * (side + (up - pltpu.roll(up, 1, 1)))
                if s < 2:
                    new[x, r : r + 8, :] = t
                else:
                    out[x - 3, :, :] = t[0:6, 0:24]
        old, new = new, old


def force_kernel(
    tab_h, w_h, jf_h, tj_h, key_h, ti_h, pv_h, heat_h, vel_h, temp,
    tab, wb, jf, tj, key, ti, pv, heat, vel, fg, fx, fy, fz, last, old, new, insem, outsem, wsem,
):
    def loaded(g):
        part = pl.ds(g * CHUNK, CHUNK)
        return pltpu.make_async_copy(w_h.at[part], wb.at[part], wsem.at[g])

    loads = [
        pltpu.make_async_copy(src, dst, insem.at[n])
        for n, (src, dst) in enumerate(
            (
                (tab_h, tab), (heat_h, heat), (tj_h, tj.at[:, 8:16]), (ti_h, ti),
                (jf_h.at[0:3], jf), (key_h, key), (pv_h, pv),
            )
        )
    ]
    loads[0].start()
    loaded(0).start()
    for c in loads[1:]:
        c.start()
    loads[0].wait()
    count = tab[5, 0]
    groups = (count + CHUNK - 1) // CHUNK

    def fetch(g, carry):
        loaded(g).start()
        return carry

    lax.fori_loop(1, groups, fetch, 0)
    none = jnp.zeros((8, 128), f32)
    for col in range(16):
        tj[col, 0:8, :] = none
        tj[col, 16:24, :] = none
    loads[1].wait()
    diffuse(heat, temp, old, new)
    for c in loads[2:]:
        c.wait()
    sums = (fg, fx, fy, fz)

    def settle(i):
        for u in range(STEP):
            row = tab[3, i * STEP + u]
            for k in range(2):
                for n, f in enumerate(sums):
                    f[pl.ds(row + 8 * k, 8), :] = wide(jnp.sum(last[u, 4 * k + n], axis=1, keepdims=True))

    def step(i, carry):
        settle(jnp.maximum(i - 1, 0))
        new = []
        for u in range(STEP):
            b = i * STEP + u
            low = tab[4, b]
            row = tab[3, b]
            t_own = [ti[pl.ds(row + 8 * k, 8), :] for k in range(2)]
            tot = [None] * 8
            for n, tile in enumerate(around(low)):
                other = [jf[m, pl.ds(tile, 8, stride=0), :] for m in range(3)]
                t_other = tj.at[...].reshape(16 * COLUMN, 128)[pl.ds(tile, 8, stride=0), :]
                for k in range(2):
                    w = wb[b, (n * 2 + k) * 8 : (n * 2 + k) * 8 + 8, :]
                    g = (w * w) * ((t_own[k] + t_other) - w)
                    for m, p in enumerate((g, g * other[0], g * other[1], g * other[2])):
                        at = 4 * k + m
                        tot[at] = p if tot[at] is None else tot[at] + p
            new.append(tot)
        for u in range(STEP):
            for n in range(8):
                last[u, n] = new[u][n]
        return carry

    steps = (count + STEP - 1) // STEP
    per = CHUNK // STEP

    def group(g, carry):
        loaded(g).wait()
        return lax.fori_loop(g * per, jnp.minimum(g * per + per, steps), step, carry)

    last[...] = jnp.zeros_like(last)
    lax.fori_loop(0, groups, group, 0)
    settle(steps - 1)

    match = matcher(key)

    def finish(item, tile, octant, k, lanes):
        row = tab[0, item] + k * 8
        hit = match(tile, octant, k)
        return tuple(
            part + jnp.where(hit, f[pl.ds(row, 8), :], 0.0)
            for part, f in zip(lanes, sums, strict=True)
        )

    def put(tile, lanes):
        total = [jnp.sum(part, axis=0, keepdims=True) for part in lanes]
        at = own_tile(tile)
        live = key[pl.ds(tile, 1), :] >= 0
        for n in range(3):
            pull = jf[n, pl.ds(at, 1), :] * total[0] - total[n + 1]
            vel[n, pl.ds(tile, 1), :] = jnp.where(live, pv[n, pl.ds(tile, 1), :] + pull * (-2.4 / ROOT), 0.0)

    over_tiles(tab, finish, put, (none,) * 4)
    out = pltpu.make_async_copy(vel, vel_h, outsem.at[0])
    out.start()
    out.wait()


VMEM = pl.BlockSpec(memory_space=pltpu.VMEM)
ANY = pl.BlockSpec(memory_space=pltpu.HBM)
LOCAL = pltpu.CompilerParams(vmem_limit_bytes=67043328)


def shape(*dims, dtype=f32):
    return jax.ShapeDtypeStruct(dims, dtype)


def vmem(like):
    return pltpu.VMEM(like.shape, like.dtype)


def meeting(n):
    return pltpu.CompilerParams(collective_id=n, has_side_effects=True, vmem_limit_bytes=67043328)


def local(positions, velocities, kicks, counts, subcell, electron_temp, laser_flux):
    order, *zeroone = static_tables()
    upper = np.triu(np.ones((128, 128)))
    bf = jnp.bfloat16
    i32 = jnp.int32
    dma = pltpu.SemaphoreType.DMA
    around8 = [dma((8,))] * 4
    tiles = shape(3, 2, 2, 8, 128)
    outs = (
        shape(4, 16 * COLUMN, 128),
        shape(TILES, 128, dtype=i32),
        shape(8, BLOCKS, dtype=i32),
        shape(2, 2, 3, 8, 128),
        shape(3, TILES, 128),
        shape(4096, 128),
    )
    jf, key, tab, heat, pv, rows = pl.pallas_call(
        gather_kernel,
        name="gather",
        out_shape=outs,
        in_specs=[ANY] * 12,
        out_specs=(ANY,) * 6,
        scratch_shapes=[
            *(vmem(tiles),) * 3,
            pltpu.VMEM((2, 2, 8), i32),
            pltpu.VMEM((2, 2, 8, 128), i32),
            pltpu.VMEM((6, 6, 24), f32),
            pltpu.SMEM((6, 6), f32),
            pltpu.VMEM((128, 128), bf),
            *(pltpu.VMEM(m.shape, bf) for m in zeroone),
            *(vmem(o) for o in outs),
            pltpu.VMEM((3, 4, 4, 8, 128), f32),
            pltpu.VMEM((8, 2, 2, 8), i32),
            pltpu.VMEM((256, 128), f32),
            pltpu.VMEM((TILES, 128), i32),
            pltpu.VMEM((8, 16, 128), f32),
            dma((12,)),
            dma((6,)),
            *around8,
        ],
        compiler_params=meeting(0),
    )(
        positions, velocities, kicks, counts, subcell, electron_temp, laser_flux,
        *(jnp.asarray(m, bf) for m in (upper, *zeroone)),
    )
    order = jnp.asarray(order)
    row = shape(ROWS, 128)
    w, ti, tl = pl.pallas_call(
        density_kernel,
        name="density",
        out_shape=(shape(BLOCKS, 128, 128), row, shape(TILES, 128)),
        in_specs=[ANY] * 5,
        out_specs=(ANY,) * 3,
        scratch_shapes=[
            pltpu.SMEM((8, BLOCKS), i32),
            pltpu.SMEM((256,), i32),
            vmem(outs[0]),
            vmem(outs[1]),
            vmem(row),
            vmem(row),
            vmem(row),
            pltpu.VMEM((TILES, 128), f32),
            pltpu.VMEM((BLOCKS, 128, 128), f32),
            pltpu.VMEM((STEP, 8, 8, 128), f32),
            pltpu.VMEM((STEP, 2, 8, 128), f32),
            dma((5,)),
            dma((2,)),
            dma((BLOCKS // CHUNK,)),
        ],
        compiler_params=LOCAL,
    )(tab, order, jf, key, rows)
    t_all, heat = pl.pallas_call(
        exchange_kernel,
        name="exchange",
        out_shape=(shape(4, 4, 8, 128), shape(4, 4, 3, 8, 128)),
        in_specs=[ANY] * 2,
        out_specs=(ANY,) * 2,
        scratch_shapes=[dma((2,)), *around8],
        compiler_params=meeting(1),
    )(tl.reshape(2, 2, 8, 128), heat)
    vel, temp = pl.pallas_call(
        force_kernel,
        name="force",
        out_shape=(shape(3, TILES, 128), shape(6, 6, 24)),
        in_specs=[ANY] * 8,
        out_specs=(ANY, VMEM),
        scratch_shapes=[
            pltpu.SMEM((8, BLOCKS), i32),
            pltpu.VMEM((BLOCKS, 128, 128), f32),
            pltpu.VMEM((3, 16 * COLUMN, 128), f32),
            pltpu.VMEM((16, COLUMN, 128), f32),
            vmem(outs[1]),
            vmem(row),
            vmem(outs[4]),
            pltpu.VMEM((4, 4, 3, 8, 128), f32),
            vmem(outs[4]),
            *(vmem(row),) * 4,
            pltpu.VMEM((STEP, 8, 8, 128), f32),
            *(pltpu.VMEM((12, 24, 128), f32),) * 2,
            dma((7,)),
            dma((1,)),
            dma((BLOCKS // CHUNK,)),
        ],
        compiler_params=LOCAL,
    )(tab, w, jf, t_all.reshape(16, 8, 128), key, ti, pv, heat)
    return (vel.reshape(3, 2, 2, 8, 128), temp)


def solution(mesh):
    in_specs = (
        P(None, "gx", "gy", None, None),
        P(None, "gx", "gy", None, None),
        P(None, "gx", "gy", None, None),
        P("gx", "gy", None),
        P("gx", "gy", None, None),
        P("gx", "gy", None),
        P("gx", "gy"),
    )
    out_specs = (P(None, "gx", "gy", None, None), P("gx", "gy", None))
    return jax.shard_map(local, mesh=mesh, in_specs=in_specs, out_specs=out_specs, check_vma=False)
```

```python
import jax
import jax.numpy as jnp
import numpy as np
from jax import lax
from jax.experimental import pallas as pl
from jax.experimental.pallas import tpu as pltpu
from jax.sharding import PartitionSpec as P

ROOT = float(np.sqrt(5.0))
FAR = 1000.0 * ROOT
TILES = 32
RANK_KEY = 1024
FAST = 3
f32 = jnp.float32
SIDES = [(dx, dy) for dx in (-1, 0, 1) for dy in (-1, 0, 1) if (dx, dy) != (0, 0)]
COLUMN = 24
PER = 1
BLOCK = 8 * PER
BLOCKS = 608 if PER == 1 else 352
TAB = 640
ROWS = BLOCKS * BLOCK + 64
CHUNK = 32
STEP = 8 // PER
WIDE = 72 * PER


def where_of(n):
    col, o, z = n // 64, n // 8 % 8, n % 8
    ox, oy, oz = o // 4, o // 2 % 2, o % 2
    return col, o, z, ((col // 2 + ox) * 3 + (col % 2 + oy)) * 9 + z + oz


def static_tables():
    col, o, z, vertex = (np.array(k) for k in zip(*(where_of(n) for n in range(256))))
    order = np.argsort(vertex, kind="stable")
    rank = np.zeros(256, np.int64)
    rank[order] = np.arange(256)
    place = (vertex[:, None] == vertex[None, :]) & (rank[:, None] < rank[None, :])
    tile = col * 8 + z
    inside = (tile[:, None] == tile[None, :]) & (o[:, None] < o[None, :])
    same = np.eye(256, dtype=bool)
    by_item = np.concatenate([place, place[:, order], inside[:, order], same[:, order]], axis=1)
    at = vertex[:, None] == np.arange(128)[None, :]
    lower = np.arange(128)[:, None] < vertex[None, :]
    by_vertex = np.concatenate([lower, lower[:, order]], axis=1)
    source = (col[order] * 128 * 8 + z[order])[None, :].repeat(8, 0).astype(np.int32)
    return by_item, at, by_vertex, source


def span(d, sender):
    if d == 0:
        return slice(0, 2) if sender else slice(1, 3)
    if sender:
        return slice(1, 2) if d > 0 else slice(0, 1)
    return slice(0, 1) if d > 0 else slice(3, 4)


def neighbour(dx, dy):
    nx, ny = lax.axis_size("gx"), lax.axis_size("gy")
    return (
        lax.rem(lax.axis_index("gx") + dx + nx, nx),
        lax.rem(lax.axis_index("gy") + dy + ny, ny),
    )


def greet():
    barrier = pltpu.get_barrier_semaphore()
    for dx, dy in SIDES:
        pl.semaphore_signal(
            barrier, inc=1, device_id=neighbour(dx, dy), device_id_type=pl.DeviceIdType.MESH
        )
    pl.semaphore_wait(barrier, len(SIDES))


def remote(src, dst, send, recv, dx, dy):
    return pltpu.make_async_remote_copy(
        src_ref=src,
        dst_ref=dst,
        send_sem=send,
        recv_sem=recv,
        device_id=neighbour(dx, dy),
        device_id_type=pl.DeviceIdType.MESH,
    )


def iota(shape, dim):
    return lax.broadcasted_iota(jnp.int32, shape, dim)


def wide(column):
    return jnp.broadcast_to(column, (8, 128))


def gather_kernel(
    pos_h, vel_h, kick_h, cnt_h, sub_h, te_h, flux_h, upper_h, by_item_h, at_h, by_vertex_h, source_h,
    jf_h, key_h, tab_h, heat_h, pv_h, rows_h,
    pos, vel, kick, cnt, sub, te, flux, upper, by_item, at, by_vertex, source,
    jf, key, tab, heat, pv, rows,
    halo, cbuf, hot, order, feat, insem, outsem, ssem, rsem, csem, dsem,
):
    loads = [
        pltpu.make_async_copy(src, dst, insem.at[n])
        for n, (src, dst) in enumerate(
            zip(
                (cnt_h, pos_h, upper_h, sub_h, te_h, vel_h, kick_h, flux_h, by_item_h, at_h, by_vertex_h, source_h),
                (cnt, pos, upper, sub, te, vel, kick, flux, by_item, at, by_vertex, source),
                strict=True,
            )
        )
    ]
    for c in loads:
        c.start()
    greet()
    copies = []
    for n, (dx, dy) in enumerate(SIDES):
        copies.append(
            remote(
                pos_h.at[:, span(dx, True), span(dy, True)],
                halo.at[:, span(dx, False), span(dy, False)],
                ssem.at[n], rsem.at[n], dx, dy,
            )
        )
        copies.append(remote(cnt_h, cbuf.at[n], csem.at[n], dsem.at[n], dx, dy))
    for c in copies:
        c.start()
    stores = [
        pltpu.make_async_copy(src, dst, outsem.at[n])
        for n, (src, dst) in enumerate(
            zip((rows, pv, heat, key, tab, jf), (rows_h, pv_h, heat_h, key_h, tab_h, jf_h), strict=True)
        )
    ]

    lane, row = iota((8, 128), 1), iota((8, 128), 0)
    pick = iota((8, 8), 0) == iota((8, 8), 1)
    deep = row.astype(f32) - 4.0

    def alive(counts):
        column = jnp.sum(jnp.where(pick, counts.astype(f32), 0.0), axis=1, keepdims=True)
        return lane < wide(column).astype(jnp.int32)

    def features(hx, hy, xyz, live):
        first = (hx * 4 + hy) * COLUMN + 8
        out = []
        for n, off in enumerate((float(hx - 2), float(hy - 2), deep)):
            out.append(jnp.where(live, (xyz[n] + off) * ROOT, FAR))
            jf[n, first : first + 8, :] = out[n]
        jf[3, first : first + 8, :] = -(out[0] * out[0] + out[1] * out[1] + out[2] * out[2])
        return out

    for col in range(16):
        for n in range(4):
            empty = jnp.full((8, 128), FAR if n < 3 else -3.0 * FAR * FAR, f32)
            jf[n, col * COLUMN : col * COLUMN + 8, :] = empty
            jf[n, col * COLUMN + 16 : col * COLUMN + 24, :] = empty

    for c in loads[:3]:
        c.wait()
    place = iota((128, 128), 0)
    ones = jnp.ones((128, 128), jnp.bfloat16)
    for n in range(9, 16):
        feat[:, n, :] = jnp.zeros((8, 128), f32)
    for col in range(4):
        tx, ty = col // 2, col % 2
        live = alive(cnt[tx, pl.ds(ty, 8, stride=0), :])
        xyz = [pos[n, tx, ty] for n in range(3)]
        own = features(tx + 1, ty + 1, xyz, live)
        octant = sum(
            jnp.where(xyz[n] >= 0.5, s, 0) for n, s in enumerate((4, 2, 1))
        )
        octant = jnp.where(live, octant, -1)
        for o in range(8):
            hot[col * 64 + o * 8 : col * 64 + o * 8 + 8, :] = jnp.where(octant == o, 1.0, 0.0)
        mine = hot[col * 64 : col * 64 + 64, :].astype(jnp.bfloat16)
        upto = jnp.dot(mine, upper[...], preferred_element_type=f32)
        total = jnp.dot(mine, ones, preferred_element_type=f32)
        rank = jnp.zeros((8, 128), f32)
        slot = jnp.zeros((8, 128), f32)
        ahead = jnp.zeros((8, 128), f32)
        for o in range(8):
            here = upto[o * 8 : o * 8 + 8, :]
            rank = jnp.where(octant == o, here, rank)
            slot = jnp.where(octant == o, here + ahead, slot)
            ahead = ahead + total[o * 8 : o * 8 + 8, :]
        key[col * 8 : col * 8 + 8, :] = jnp.where(
            live, octant * RANK_KEY + rank.astype(jnp.int32) - 1, -1
        )
        order[col * 8 : col * 8 + 8, :] = jnp.where(live, slot.astype(jnp.int32) - 1, -1)
        for n in range(3):
            high = own[n].astype(jnp.bfloat16).astype(f32)
            rest = own[n] - high
            middle = rest.astype(jnp.bfloat16).astype(f32)
            feat[:, n, :] = high
            feat[:, 3 + n, :] = middle
            feat[:, 6 + n, :] = rest - middle
        every = feat[...].reshape(128, 128)
        block = jnp.zeros((128, 128), f32)
        for z in range(8):
            hit = order[pl.ds(col * 8 + z, 128, stride=0), :] == place
            block = block + lax.dot_general(
                jnp.where(hit, 1.0, 0.0).astype(jnp.bfloat16),
                jnp.where(lax.shift_right_logical(place, 4) == z, every, 0.0).astype(jnp.bfloat16),
                (((1,), (1,)), ((), ())),
                preferred_element_type=f32,
            )
        rows[col * 128 : col * 128 + 128, :] = block
    stores[0].start()

    for c in loads[3:8]:
        c.wait()
    for col in range(4):
        tx, ty = col // 2, col % 2
        live = alive(cnt[tx, pl.ds(ty, 8, stride=0), :])
        cell = jnp.where(live, sub[tx, ty], -1)
        te_atom = jnp.zeros((8, 128), f32)
        for a in range(3):
            for b in range(3):
                line = te[tx * 3 + a, pl.ds(ty * 3 + b, 8, stride=0), :]
                for c in range(3):
                    third = iota((8, 24), 1) == 3 * iota((8, 24), 0) + c
                    value = jnp.sum(jnp.where(third, line, 0.0), axis=1, keepdims=True)
                    te_atom = jnp.where(cell == 9 * a + 3 * b + c, wide(value), te_atom)
        sigma = jnp.sqrt(0.2 * te_atom)
        v = [vel[n, tx, ty] for n in range(3)]
        k = [kick[n, tx, ty] for n in range(3)]
        for n in range(3):
            pv[n, col * 8 : col * 8 + 8, :] = jnp.where(live, 0.9 * v[n] + sigma * k[n], 0.0)
        work = 0.1 * (v[0] * v[0] + v[1] * v[1] + v[2] * v[2]) - sigma * (
            k[0] * v[0] + k[1] * v[1] + k[2] * v[2]
        )
        depth = jnp.exp((iota((1, 128), 1).astype(f32) + 0.5) * (-1.0 / 38.0)) * 0.05
        for a in range(3):
            for b in range(3):
                grid = jnp.zeros((8, 128), f32)
                for c in range(3):
                    part = jnp.where(cell == 9 * a + 3 * b + c, work, 0.0)
                    value = wide(jnp.sum(part, axis=1, keepdims=True))
                    grid = jnp.where(lane == 3 * row + c, value, grid)
                gained = jnp.sum(grid, axis=0, keepdims=True)
                base = te[tx * 3 + a, ty * 3 + b : ty * 3 + b + 1, :]
                light = flux[tx * 3 + a, ty * 3 + b] * depth
                heat[tx, ty, a, b : b + 1, :] = gained * (1.0 / 40.0) + light
                heat[tx, ty, a, b : b + 1, 0:24] = heat[tx, ty, a, b : b + 1, 0:24] + base
        for a in range(3):
            heat[tx, ty, a, 3:8, :] = jnp.zeros((5, 128), f32)
    for c in stores[1:4]:
        c.start()

    for c in loads[8:]:
        c.wait()
    bf = jnp.bfloat16
    both = (((1,), (1,)), ((), ()))
    count = lax.dot_general(ones[0:8], hot[...].astype(bf), both, preferred_element_type=f32)
    few = count.astype(bf)
    sums = jnp.dot(few, by_item[...], preferred_element_type=f32).astype(jnp.int32)
    many = jnp.dot(few, at[...], preferred_element_type=f32)
    blocks = lax.shift_right_logical(many.astype(jnp.int32) + (BLOCK - 1), 3 if PER == 1 else 4)
    blocks = blocks.astype(f32)
    begin = jnp.dot(blocks.astype(bf), by_vertex[...], preferred_element_type=f32).astype(jnp.int32) * BLOCK
    number = count.astype(jnp.int32)
    lined = sums[:, 768:1024]

    def widest(values, shifts):
        for s in shifts:
            values = jnp.maximum(values, pltpu.roll(values, 256 - s, 1))
        return values

    table = (
        sums[:, 0:256] + begin[:, 0:256],
        number,
        widest(number, (8, 16, 32)),
        sums[:, 512:768] * 8 + source[...],
        sums[:, 256:512] + begin[:, 256:512],
        lined,
        widest(lined, (1, 2, 4)),
    )
    for n, values in enumerate(table):
        tab[n : n + 1, 0:256] = values[0:1, :]
    rep = jnp.broadcast_to(blocks[0:1, :], (128, 128)).astype(bf)
    under = jnp.where(iota((128, 128), 1) < place, 1.0, 0.0).astype(bf)
    upon = jnp.where(iota((128, 128), 1) <= place, 1.0, 0.0).astype(bf)
    low_block = lax.dot_general(under, rep, both, preferred_element_type=f32)
    top_block = lax.dot_general(upon, rep, both, preferred_element_type=f32)
    for n in range(8):
        tab[n : n + 1, 256:TAB] = jnp.broadcast_to(top_block[127:128, 0:1], (1, TAB - 256)).astype(jnp.int32)
    lows = []
    for r in range(11):
        base_tile = jnp.zeros((8, 128), f32)
        for s in range(8):
            v = r * 8 + s
            if v < 81:
                c = v // 9
                base_tile = jnp.where(row == s, float(((c // 3) * 4 + c % 3) * COLUMN + 7 + v % 9), base_tile)
        lows.append(base_tile)
    for j in range(TAB // 128):
        b = (lane + 128 * j).astype(f32)
        low = jnp.zeros((8, 128), f32)
        for r in range(11):
            lo, hi = low_block[r * 8 : r * 8 + 8, :], top_block[r * 8 : r * 8 + 8, :]
            low = low + jnp.where((lo <= b) & (b < hi), lows[r], 0.0)
        tab[7:8, j * 128 : j * 128 + 128] = jnp.sum(low, axis=0, keepdims=True).astype(jnp.int32)
    stores[4].start()

    for c in copies:
        c.wait()
    for n, (dx, dy) in enumerate(SIDES):
        for hx in range(4)[span(dx, False)]:
            for hy in range(4)[span(dy, False)]:
                sx = hx - 1 if dx == 0 else (1 if dx > 0 else 0)
                sy = hy - 1 if dy == 0 else (1 if dy > 0 else 0)
                live = alive(cbuf[n, sx, pl.ds(sy, 8, stride=0), :])
                features(hx, hy, [halo[m, hx, hy] for m in range(3)], live)
    stores[5].start()
    for c in stores:
        c.wait()


def exchange_kernel(t, heat, t_all, heat_all, own, ssem, rsem, csem, dsem):
    mine = [
        pltpu.make_async_copy(t, t_all.at[1:3, 1:3], own.at[0]),
        pltpu.make_async_copy(heat, heat_all.at[1:3, 1:3], own.at[1]),
    ]
    for c in mine:
        c.start()
    greet()
    copies = []
    for n, (dx, dy) in enumerate(SIDES):
        sx, sy, rx, ry = span(dx, True), span(dy, True), span(dx, False), span(dy, False)
        copies.append(remote(t.at[sx, sy], t_all.at[rx, ry], ssem.at[n], rsem.at[n], dx, dy))
        copies.append(remote(heat.at[sx, sy], heat_all.at[rx, ry], csem.at[n], dsem.at[n], dx, dy))
    for c in copies:
        c.start()
    for c in mine + copies:
        c.wait()


def own_tile(tile):
    return (tile // 16 + 1) * (4 * COLUMN) + (tile // 8 % 2 + 1) * COLUMN + tile % 8 + 8


def pack_rows(tab, rows, packed):
    part = lax.shift_right_logical(iota((8, 128), 1), 4)

    def step(i, carry):
        widest = tab[6, i * 8]

        def move(u, k):
            code, dst = tab[3, i * 8 + u], tab[4, i * 8 + u]
            src = lax.shift_right_logical(code, 3)
            value = rows[pl.ds(src + 8 * k, 8), :]
            packed[pl.ds(dst + 8 * k, 8), :] = jnp.where(part == (code & 7), value, 0.0)

        @pl.when(widest <= FAST * 8)
        def _():
            for u in range(8):
                for k in range(FAST):
                    move(u, k)

        @pl.when(widest > FAST * 8)
        def _():
            def one(u, carry):
                def inner(k, carry):
                    move(u, k)
                    return carry

                return lax.fori_loop(0, (tab[5, i * 8 + u] + 7) // 8, inner, carry)

            lax.fori_loop(0, 8, one, 0)

        return carry

    lax.fori_loop(0, 32, step, 0)


def over_tiles(tab, chunk, put, zero):
    def step(tile, carry):
        first = tile // 8 * 64 + tile % 8
        widest = tab[2, first]

        @pl.when(widest <= FAST * 8)
        def _():
            lanes = zero
            for o in range(8):
                for k in range(FAST):
                    lanes = chunk(first + o * 8, tile, o, k, lanes)
            put(tile, lanes)

        @pl.when(widest > FAST * 8)
        def _():
            def per(o, lanes):
                item = first + o * 8

                def inner(k, lanes):
                    return chunk(item, tile, o, k, lanes)

                return lax.fori_loop(0, (tab[1, item] + 7) // 8, inner, lanes)

            put(tile, lax.fori_loop(0, 8, per, zero))

        return carry

    lax.fori_loop(0, TILES, step, 0)


def around(low):
    return [low + (dx * 4 + dy) * COLUMN + dz for dx in (0, 1) for dy in (0, 1) for dz in (0, 1)]


def matcher(key):
    sub = iota((8, 128), 0)

    def match(tile, octant, k):
        return key[pl.ds(tile, 8, stride=0), :] == sub + (octant * RANK_KEY + k * 8)

    return match


def slope_of(tot):
    return wide(0.1875 + 0.625 * lax.rsqrt(jnp.sum(tot, axis=1, keepdims=True)))


def density_kernel(
    tab_h, jf_h, key_h, rows_h, w_h, tl_h,
    tab, jf, key, rows, packed, ti, tl, wb, own, last, insem, outsem, wsem,
):
    loads = [
        pltpu.make_async_copy(src, dst, insem.at[n])
        for n, (src, dst) in enumerate(((tab_h, tab), (rows_h, rows.at[0:512]), (jf_h, jf), (key_h, key)))
    ]
    for c in loads:
        c.start()
    for c in loads[:2]:
        c.wait()
    pack_rows(tab, rows, packed)
    for c in loads[2:]:
        c.wait()
    count = tab[0, 256]
    feature = iota((8, 128), 1) & 15
    masks = [(feature == n) | (feature == n + 3) | (feature == n + 6) for n in range(3)]

    def own_rows(b):
        out = []
        for k in range(PER):
            value = packed[pl.ds(pl.multiple_of(b * BLOCK + 8 * k, 8), 8), :]
            x, y, z = (wide(jnp.sum(jnp.where(m, value, 0.0), axis=1, keepdims=True)) for m in masks)
            out += [x + x, y + y, z + z, 1.0 - (x * x + y * y + z * z)]
        return out

    def keep(blocks):
        for u, values in enumerate(blocks):
            for n, value in enumerate(values):
                own[u, n] = value

    def settle(i, tots):
        for u in range(STEP):
            b = i * STEP + u
            for k in range(PER):
                t = slope_of(tots[u][k])
                ti[pl.ds(pl.multiple_of(b * BLOCK + 8 * k, 8), 8), :] = t
                wb[b, (8 * PER + k) * 8 : (8 * PER + k) * 8 + 8, :] = t

    def step(i, carry):
        tots = [[last[u, k] for k in range(PER)] for u in range(STEP)]
        ahead = [own_rows(jnp.minimum((i + 1) * STEP + u, BLOCKS - 1)) for u in range(STEP)]
        new = []
        for u in range(STEP):
            b = i * STEP + u
            mine = [[own[u, 4 * k + n] for n in range(4)] for k in range(PER)]
            tot = [None] * PER
            for n, tile in enumerate(around(tab[7, b])):
                xj, yj, zj, bj = (jf[m, pl.ds(tile, 8, stride=0), :] for m in range(4))
                for k in range(PER):
                    x, y, z, a = mine[k]
                    w = jnp.maximum((a + bj) + (x * xj + y * yj + z * zj), 0.0)
                    wb[b, (n * PER + k) * 8 : (n * PER + k) * 8 + 8, :] = w
                    cube = w * w * w
                    tot[k] = cube if tot[k] is None else tot[k] + cube
            new.append(tot)
        settle(jnp.maximum(i - 1, 0), tots)
        keep(ahead)
        for u in range(STEP):
            for k in range(PER):
                last[u, k] = new[u][k]
        return carry

    def saved(g):
        part = pl.ds(g * CHUNK, CHUNK)
        return pltpu.make_async_copy(wb.at[part], w_h.at[part], wsem.at[g])

    steps = (count + STEP - 1) // STEP
    groups = (count + CHUNK - 1) // CHUNK
    per = CHUNK // STEP

    def group(g, carry):
        lax.fori_loop(g * per, jnp.minimum(g * per + per, steps), step, 0)

        @pl.when(g > 0)
        def _():
            saved(g - 1).start()

        return carry

    keep([own_rows(u) for u in range(STEP)])
    last[...] = jnp.ones_like(last)
    lax.fori_loop(0, groups, group, 0)
    settle(steps - 1, [[last[u, k] for k in range(PER)] for u in range(STEP)])
    saved(groups - 1).start()

    match = matcher(key)

    def finish(item, tile, octant, k, lanes):
        t = ti[pl.ds(tab[0, item] + k * 8, 8), :]
        return lanes + jnp.where(match(tile, octant, k), t, 0.0)

    def put(tile, lanes):
        tl[pl.ds(tile, 1), :] = jnp.sum(lanes, axis=0, keepdims=True)

    over_tiles(tab, finish, put, jnp.zeros((8, 128), f32))
    lanes_out = pltpu.make_async_copy(tl, tl_h, outsem.at[0])
    lanes_out.start()

    def drain(g, carry):
        saved(g).wait()
        return carry

    lax.fori_loop(0, groups, drain, 0)
    lanes_out.wait()


def diffuse(heat, out, old, new):
    for x in range(12):
        for y in range(4):
            old[x, y * 3 : y * 3 + 8, :] = heat[x // 3, y, x % 3]
    lane = iota((8, 128), 1)
    for s in range(3):
        for x in range(s + 1, 11 - s):
            for r in (1, 9) if s == 0 else (s + 1,):
                t = old[x, r : r + 8, :]
                near = [old[x - 1, r : r + 8, :], old[x + 1, r : r + 8, :], old[x, r - 1 : r + 7, :], old[x, r + 1 : r + 9, :]]
                q = t * t
                side = near[0] * near[0] + near[1] * near[1] + near[2] * near[2] + near[3] * near[3] - 4.0 * q
                up = jnp.where(lane < 23, pltpu.roll(q, 127, 1) - q, 0.0)
                t = t + 0.025 * (side + (up - pltpu.roll(up, 1, 1)))
                if s < 2:
                    new[x, r : r + 8, :] = t
                else:
                    out[x - 3, :, :] = t[0:6, 0:24]
        old, new = new, old


def force_kernel(
    tab_h, w_h, jf_h, tj_h, key_h, pv_h, heat_h, vel_h, temp_h,
    tab, wb, jf, tj, key, pv, heat, vel, temp, fg, fx, fy, fz, last, old, new, insem, outsem, wsem,
):
    def loaded(g):
        part = pl.ds(g * CHUNK, CHUNK)
        return pltpu.make_async_copy(w_h.at[part], wb.at[part], wsem.at[g])

    loads = [
        pltpu.make_async_copy(src, dst, insem.at[n])
        for n, (src, dst) in enumerate(
            (
                (tab_h, tab), (heat_h, heat), (tj_h, tj.at[:, 8:16]),
                (jf_h.at[0:3], jf), (key_h, key), (pv_h, pv),
            )
        )
    ]
    loads[0].start()
    loaded(0).start()
    for c in loads[1:]:
        c.start()
    loads[0].wait()
    count = tab[0, 256]
    groups = (count + CHUNK - 1) // CHUNK

    def fetch(g, carry):
        loaded(g).start()
        return carry

    lax.fori_loop(1, groups, fetch, 0)
    none = jnp.zeros((8, 128), f32)
    for col in range(16):
        tj[col, 0:8, :] = none
        tj[col, 16:24, :] = none
    loads[1].wait()
    diffuse(heat, temp, old, new)
    warm = pltpu.make_async_copy(temp, temp_h, outsem.at[1])
    warm.start()
    for c in loads[2:]:
        c.wait()
    sums = (fg, fx, fy, fz)

    def settle(i):
        for u in range(STEP):
            row = (i * STEP + u) * BLOCK
            for k in range(PER):
                for n, f in enumerate(sums):
                    at = pl.ds(pl.multiple_of(row + 8 * k, 8), 8)
                    f[at, :] = wide(jnp.sum(last[u, 4 * k + n], axis=1, keepdims=True))

    def step(i, carry):
        settle(jnp.maximum(i - 1, 0))
        new = []
        for u in range(STEP):
            b = i * STEP + u
            t_own = [wb[b, (8 * PER + k) * 8 : (8 * PER + k) * 8 + 8, :] for k in range(PER)]
            tot = [None] * (4 * PER)
            for n, tile in enumerate(around(tab[7, b])):
                other = [jf[m, pl.ds(tile, 8, stride=0), :] for m in range(3)]
                t_other = tj.at[...].reshape(16 * COLUMN, 128)[pl.ds(tile, 8, stride=0), :]
                for k in range(PER):
                    w = wb[b, (n * PER + k) * 8 : (n * PER + k) * 8 + 8, :]
                    g = (w * w) * ((t_own[k] + t_other) - w)
                    for m, p in enumerate((g, g * other[0], g * other[1], g * other[2])):
                        at = 4 * k + m
                        tot[at] = p if tot[at] is None else tot[at] + p
            new.append(tot)
        for u in range(STEP):
            for n in range(4 * PER):
                last[u, n] = new[u][n]
        return carry

    steps = (count + STEP - 1) // STEP
    per = CHUNK // STEP

    def group(g, carry):
        loaded(g).wait()
        return lax.fori_loop(g * per, jnp.minimum(g * per + per, steps), step, carry)

    last[...] = jnp.zeros_like(last)
    lax.fori_loop(0, groups, group, 0)
    settle(steps - 1)

    match = matcher(key)

    def finish(item, tile, octant, k, lanes):
        row = tab[0, item] + k * 8
        hit = match(tile, octant, k)
        return tuple(
            part + jnp.where(hit, f[pl.ds(row, 8), :], 0.0)
            for part, f in zip(lanes, sums, strict=True)
        )

    def put(tile, lanes):
        total = [jnp.sum(part, axis=0, keepdims=True) for part in lanes]
        at = own_tile(tile)
        live = key[pl.ds(tile, 1), :] >= 0
        for n in range(3):
            pull = jf[n, pl.ds(at, 1), :] * total[0] - total[n + 1]
            vel[n, pl.ds(tile, 1), :] = jnp.where(live, pv[n, pl.ds(tile, 1), :] + pull * (-2.4 / ROOT), 0.0)

    over_tiles(tab, finish, put, (none,) * 4)
    out = pltpu.make_async_copy(vel, vel_h, outsem.at[0])
    out.start()
    out.wait()
    warm.wait()


ANY = pl.BlockSpec(memory_space=pltpu.HBM)
LOCAL = pltpu.CompilerParams(vmem_limit_bytes=67043328)


def shape(*dims, dtype=f32):
    return jax.ShapeDtypeStruct(dims, dtype)


def vmem(like):
    return pltpu.VMEM(like.shape, like.dtype)


def meeting(n):
    return pltpu.CompilerParams(collective_id=n, has_side_effects=True, vmem_limit_bytes=67043328)


def local(positions, velocities, kicks, counts, subcell, electron_temp, laser_flux):
    *zeroone, source = static_tables()
    upper = np.triu(np.ones((128, 128)))
    bf = jnp.bfloat16
    i32 = jnp.int32
    dma = pltpu.SemaphoreType.DMA
    around8 = [dma((8,))] * 4
    tiles = shape(3, 2, 2, 8, 128)
    outs = (
        shape(4, 16 * COLUMN, 128),
        shape(TILES, 128, dtype=i32),
        shape(8, TAB, dtype=i32),
        shape(2, 2, 3, 8, 128),
        shape(3, TILES, 128),
        shape(512, 128),
    )
    jf, key, tab, heat, pv, rows = pl.pallas_call(
        gather_kernel,
        name="gather",
        out_shape=outs,
        in_specs=[ANY] * 12,
        out_specs=(ANY,) * 6,
        scratch_shapes=[
            *(vmem(tiles),) * 3,
            pltpu.VMEM((2, 2, 8), i32),
            pltpu.VMEM((2, 2, 8, 128), i32),
            pltpu.VMEM((6, 6, 24), f32),
            pltpu.SMEM((6, 6), f32),
            pltpu.VMEM((128, 128), bf),
            *(pltpu.VMEM(m.shape, bf) for m in zeroone),
            pltpu.VMEM(source.shape, i32),
            *(vmem(o) for o in outs),
            pltpu.VMEM((3, 4, 4, 8, 128), f32),
            pltpu.VMEM((8, 2, 2, 8), i32),
            pltpu.VMEM((256, 128), f32),
            pltpu.VMEM((TILES, 128), i32),
            pltpu.VMEM((8, 16, 128), f32),
            dma((12,)),
            dma((6,)),
            *around8,
        ],
        compiler_params=meeting(0),
    )(
        positions, velocities, kicks, counts, subcell, electron_temp, laser_flux,
        *(jnp.asarray(m, bf) for m in (upper, *zeroone)), jnp.asarray(source),
    )
    row = shape(ROWS, 128)
    saved = shape(BLOCKS, WIDE, 128)
    w, tl = pl.pallas_call(
        density_kernel,
        name="density",
        out_shape=(saved, shape(TILES, 128)),
        in_specs=[ANY] * 4,
        out_specs=(ANY,) * 2,
        scratch_shapes=[
            pltpu.SMEM((8, TAB), i32),
            vmem(outs[0]),
            vmem(outs[1]),
            pltpu.VMEM((1024, 128), f32),
            vmem(row),
            vmem(row),
            pltpu.VMEM((TILES, 128), f32),
            vmem(saved),
            pltpu.VMEM((STEP, 4 * PER, 8, 128), f32),
            pltpu.VMEM((STEP, PER, 8, 128), f32),
            dma((4,)),
            dma((1,)),
            dma((BLOCKS // CHUNK,)),
        ],
        compiler_params=LOCAL,
    )(tab, jf, key, rows)
    t_all, heat = pl.pallas_call(
        exchange_kernel,
        name="exchange",
        out_shape=(shape(4, 4, 8, 128), shape(4, 4, 3, 8, 128)),
        in_specs=[ANY] * 2,
        out_specs=(ANY,) * 2,
        scratch_shapes=[dma((2,)), *around8],
        compiler_params=meeting(1),
    )(tl.reshape(2, 2, 8, 128), heat)
    vel, temp = pl.pallas_call(
        force_kernel,
        name="force",
        out_shape=(shape(3, TILES, 128), shape(6, 6, 24)),
        in_specs=[ANY] * 7,
        out_specs=(ANY,) * 2,
        scratch_shapes=[
            pltpu.SMEM((8, TAB), i32),
            vmem(saved),
            pltpu.VMEM((3, 16 * COLUMN, 128), f32),
            pltpu.VMEM((16, COLUMN, 128), f32),
            vmem(outs[1]),
            vmem(outs[4]),
            pltpu.VMEM((4, 4, 3, 8, 128), f32),
            vmem(outs[4]),
            pltpu.VMEM((6, 6, 24), f32),
            *(vmem(row),) * 4,
            pltpu.VMEM((STEP, 4 * PER, 8, 128), f32),
            *(pltpu.VMEM((12, 24, 128), f32),) * 2,
            dma((6,)),
            dma((2,)),
            dma((BLOCKS // CHUNK,)),
        ],
        compiler_params=LOCAL,
    )(tab, w, jf, t_all.reshape(16, 8, 128), key, pv, heat)
    return (vel.reshape(3, 2, 2, 8, 128), temp)


def solution(mesh):
    in_specs = (
        P(None, "gx", "gy", None, None),
        P(None, "gx", "gy", None, None),
        P(None, "gx", "gy", None, None),
        P("gx", "gy", None),
        P("gx", "gy", None, None),
        P("gx", "gy", None),
        P("gx", "gy"),
    )
    out_specs = (P(None, "gx", "gy", None, None), P("gx", "gy", None))
    return jax.shard_map(local, mesh=mesh, in_specs=in_specs, out_specs=out_specs, check_vma=False)
```

```python
import jax
import jax.numpy as jnp
import numpy as np
from jax import lax
from jax.experimental import pallas as pl
from jax.experimental.pallas import tpu as pltpu
from jax.sharding import PartitionSpec as P

ROOT = float(np.sqrt(5.0))
FAR = 1000.0 * ROOT
TILES = 32
RANK_KEY = 1024
FAST = (0, 2, 3)
f32 = jnp.float32
SIDES = [(dx, dy) for dx in (-1, 0, 1) for dy in (-1, 0, 1) if (dx, dy) != (0, 0)]
COLUMN = 24
PER = 1
BLOCK = 8 * PER
BLOCKS = 608 if PER == 1 else 352
ROWS = BLOCKS * BLOCK + 64
CHUNK = 32
GROUP = 8
STEP = 8 // PER
WIDE = 72 * PER


def where_of(n):
    col, o, z = n // 64, n // 8 % 8, n % 8
    ox, oy, oz = o // 4, o // 2 % 2, o % 2
    return col, o, z, ((col // 2 + ox) * 3 + (col % 2 + oy)) * 9 + z + oz


def static_tables():
    col, o, z, vertex = (np.array(k) for k in zip(*(where_of(n) for n in range(256))))
    order = np.argsort(vertex, kind="stable")
    rank = np.zeros(256, np.int64)
    rank[order] = np.arange(256)
    place = (vertex[:, None] == vertex[None, :]) & (rank[:, None] < rank[None, :])
    tile = col * 8 + z
    inside = (tile[:, None] == tile[None, :]) & (o[:, None] < o[None, :])
    same = np.eye(256, dtype=bool)
    by_item = np.concatenate([place, place[:, order], inside[:, order], same[:, order]], axis=1)
    at = vertex[:, None] == np.arange(128)[None, :]
    lower = np.arange(128)[:, None] < vertex[None, :]
    by_vertex = np.concatenate([lower, lower[:, order]], axis=1)
    source = (col[order] * 128 * 8 + z[order])[None, :].repeat(8, 0).astype(np.int32)
    return by_item, at, by_vertex, source


def span(d, sender):
    if d == 0:
        return slice(0, 2) if sender else slice(1, 3)
    if sender:
        return slice(1, 2) if d > 0 else slice(0, 1)
    return slice(0, 1) if d > 0 else slice(3, 4)


def neighbour(dx, dy):
    nx, ny = lax.axis_size("gx"), lax.axis_size("gy")
    return (
        lax.rem(lax.axis_index("gx") + dx + nx, nx),
        lax.rem(lax.axis_index("gy") + dy + ny, ny),
    )


def greet():
    barrier = pltpu.get_barrier_semaphore()
    for dx, dy in SIDES:
        pl.semaphore_signal(
            barrier, inc=1, device_id=neighbour(dx, dy), device_id_type=pl.DeviceIdType.MESH
        )
    pl.semaphore_wait(barrier, len(SIDES))


def remote(src, dst, send, recv, dx, dy):
    return pltpu.make_async_remote_copy(
        src_ref=src,
        dst_ref=dst,
        send_sem=send,
        recv_sem=recv,
        device_id=neighbour(dx, dy),
        device_id_type=pl.DeviceIdType.MESH,
    )


def iota(shape, dim):
    return lax.broadcasted_iota(jnp.int32, shape, dim)


def wide(column):
    return jnp.broadcast_to(column, (8, 128))


def alive_of(counts):
    pick = iota((8, 8), 0) == iota((8, 8), 1)
    column = jnp.sum(jnp.where(pick, counts.astype(f32), 0.0), axis=1, keepdims=True)
    return iota((8, 128), 1) < wide(column).astype(jnp.int32)


def features_of(hx, hy, xyz, live):
    deep = iota((8, 128), 0).astype(f32) - 4.0
    return [
        jnp.where(live, (xyz[n] + off) * ROOT, FAR)
        for n, off in enumerate((float(hx - 2), float(hy - 2), deep))
    ]


def gather_kernel(
    pos_h, vel_h, kick_h, cnt_h, sub_h, te_h, flux_h, upper_h, by_item_h, at_h, by_vertex_h, source_h,
    halo, cbuf, key_h, tab_h, heat_h, pv_h, rows_h,
    pos, vel, kick, cnt, sub, te, flux, upper, by_item, at, by_vertex, source,
    key, tab, heat, pv, rows, hot, order, feat, insem, outsem, ssem, rsem, csem, dsem,
):
    loads = [
        pltpu.make_async_copy(src, dst, insem.at[n])
        for n, (src, dst) in enumerate(
            zip(
                (cnt_h, pos_h, upper_h, sub_h, te_h, vel_h, kick_h, flux_h, by_item_h, at_h, by_vertex_h, source_h),
                (cnt, pos, upper, sub, te, vel, kick, flux, by_item, at, by_vertex, source),
                strict=True,
            )
        )
    ]
    for c in loads:
        c.start()
    greet()
    copies = []
    for n, (dx, dy) in enumerate(SIDES):
        copies.append(
            remote(
                pos_h.at[:, span(dx, True), span(dy, True)],
                halo.at[:, span(dx, False), span(dy, False)],
                ssem.at[n], rsem.at[n], dx, dy,
            )
        )
        copies.append(remote(cnt_h, cbuf.at[n], csem.at[n], dsem.at[n], dx, dy))
    for c in copies:
        c.start()
    stores = [
        pltpu.make_async_copy(src, dst, outsem.at[n])
        for n, (src, dst) in enumerate(
            zip((rows, pv, heat, key, tab), (rows_h, pv_h, heat_h, key_h, tab_h), strict=True)
        )
    ]

    lane, row = iota((8, 128), 1), iota((8, 128), 0)
    for c in loads[:3]:
        c.wait()
    place = iota((128, 128), 0)
    ones = jnp.ones((128, 128), jnp.bfloat16)
    for n in range(9, 16):
        feat[:, n, :] = jnp.zeros((8, 128), f32)
    for col in range(4):
        tx, ty = col // 2, col % 2
        live = alive_of(cnt[tx, pl.ds(ty, 8, stride=0), :])
        xyz = [pos[n, tx, ty] for n in range(3)]
        own = features_of(tx + 1, ty + 1, xyz, live)
        octant = sum(
            jnp.where(xyz[n] >= 0.5, s, 0) for n, s in enumerate((4, 2, 1))
        )
        octant = jnp.where(live, octant, -1)
        for o in range(8):
            hot[col * 64 + o * 8 : col * 64 + o * 8 + 8, :] = jnp.where(octant == o, 1.0, 0.0)
        mine = hot[col * 64 : col * 64 + 64, :].astype(jnp.bfloat16)
        upto = jnp.dot(mine, upper[...], preferred_element_type=f32)
        total = jnp.dot(mine, ones, preferred_element_type=f32)
        rank = jnp.zeros((8, 128), f32)
        slot = jnp.zeros((8, 128), f32)
        ahead = jnp.zeros((8, 128), f32)
        for o in range(8):
            here = upto[o * 8 : o * 8 + 8, :]
            rank = jnp.where(octant == o, here, rank)
            slot = jnp.where(octant == o, here + ahead, slot)
            ahead = ahead + total[o * 8 : o * 8 + 8, :]
        key[col * 8 : col * 8 + 8, :] = jnp.where(
            live, octant * RANK_KEY + rank.astype(jnp.int32) - 1, -1
        )
        order[col * 8 : col * 8 + 8, :] = jnp.where(live, slot.astype(jnp.int32) - 1, -1)
        for n in range(3):
            high = own[n].astype(jnp.bfloat16).astype(f32)
            rest = own[n] - high
            middle = rest.astype(jnp.bfloat16).astype(f32)
            feat[:, n, :] = high
            feat[:, 3 + n, :] = middle
            feat[:, 6 + n, :] = rest - middle
        every = feat[...].reshape(128, 128)
        block = jnp.zeros((128, 128), f32)
        for z in range(8):
            hit = order[pl.ds(col * 8 + z, 128, stride=0), :] == place
            block = block + lax.dot_general(
                jnp.where(hit, 1.0, 0.0).astype(jnp.bfloat16),
                jnp.where(lax.shift_right_logical(place, 4) == z, every, 0.0).astype(jnp.bfloat16),
                (((1,), (1,)), ((), ())),
                preferred_element_type=f32,
            )
        rows[col * 128 : col * 128 + 128, :] = block
    stores[0].start()

    for c in loads[3:8]:
        c.wait()
    for col in range(4):
        tx, ty = col // 2, col % 2
        live = alive_of(cnt[tx, pl.ds(ty, 8, stride=0), :])
        cell = jnp.where(live, sub[tx, ty], -1)
        te_atom = jnp.zeros((8, 128), f32)
        for a in range(3):
            for b in range(3):
                line = te[tx * 3 + a, pl.ds(ty * 3 + b, 8, stride=0), :]
                for c in range(3):
                    third = iota((8, 24), 1) == 3 * iota((8, 24), 0) + c
                    value = jnp.sum(jnp.where(third, line, 0.0), axis=1, keepdims=True)
                    te_atom = jnp.where(cell == 9 * a + 3 * b + c, wide(value), te_atom)
        sigma = jnp.sqrt(0.2 * te_atom)
        v = [vel[n, tx, ty] for n in range(3)]
        k = [kick[n, tx, ty] for n in range(3)]
        for n in range(3):
            pv[n, col * 8 : col * 8 + 8, :] = jnp.where(live, 0.9 * v[n] + sigma * k[n], 0.0)
        work = 0.1 * (v[0] * v[0] + v[1] * v[1] + v[2] * v[2]) - sigma * (
            k[0] * v[0] + k[1] * v[1] + k[2] * v[2]
        )
        depth = jnp.exp((iota((1, 128), 1).astype(f32) + 0.5) * (-1.0 / 38.0)) * 0.05
        for a in range(3):
            for b in range(3):
                grid = jnp.zeros((8, 128), f32)
                for c in range(3):
                    part = jnp.where(cell == 9 * a + 3 * b + c, work, 0.0)
                    value = wide(jnp.sum(part, axis=1, keepdims=True))
                    grid = jnp.where(lane == 3 * row + c, value, grid)
                gained = jnp.sum(grid, axis=0, keepdims=True)
                base = te[tx * 3 + a, ty * 3 + b : ty * 3 + b + 1, :]
                light = flux[tx * 3 + a, ty * 3 + b] * depth
                heat[tx, ty, a, b : b + 1, :] = gained * (1.0 / 40.0) + light
                heat[tx, ty, a, b : b + 1, 0:24] = heat[tx, ty, a, b : b + 1, 0:24] + base
        for a in range(3):
            heat[tx, ty, a, 3:8, :] = jnp.zeros((5, 128), f32)
    for c in stores[1:4]:
        c.start()

    for c in loads[8:]:
        c.wait()
    bf = jnp.bfloat16
    both = (((1,), (1,)), ((), ()))
    count = lax.dot_general(ones[0:8], hot[...].astype(bf), both, preferred_element_type=f32)
    few = count.astype(bf)
    sums = jnp.dot(few, by_item[...], preferred_element_type=f32).astype(jnp.int32)
    many = jnp.dot(few, at[...], preferred_element_type=f32)
    blocks = lax.shift_right_logical(many.astype(jnp.int32) + (BLOCK - 1), 3 if PER == 1 else 4)
    blocks = blocks.astype(f32)
    begin = jnp.dot(blocks.astype(bf), by_vertex[...], preferred_element_type=f32).astype(jnp.int32) * BLOCK
    number = count.astype(jnp.int32)
    lined = sums[:, 768:1024]

    def widest(values, shifts):
        for s in shifts:
            values = jnp.maximum(values, pltpu.roll(values, 256 - s, 1))
        return values

    rep = jnp.broadcast_to(blocks[0:1, :], (128, 128)).astype(bf)
    under = jnp.where(iota((128, 128), 1) < place, 1.0, 0.0).astype(bf)
    upon = jnp.where(iota((128, 128), 1) <= place, 1.0, 0.0).astype(bf)
    low_block = lax.dot_general(under, rep, both, preferred_element_type=f32)
    top_block = lax.dot_general(upon, rep, both, preferred_element_type=f32)
    lows = []
    for r in range(11):
        base_tile = jnp.zeros((8, 128), f32)
        for s in range(8):
            v = r * 8 + s
            if v < 81:
                c = v // 9
                base_tile = jnp.where(row == s, float(((c // 3) * 4 + c % 3) * COLUMN + 7 + v % 9), base_tile)
        lows.append(base_tile)
    lowest = []
    for j in range(6):
        b = (lane + 128 * j).astype(f32)
        low = jnp.zeros((8, 128), f32)
        for r in range(11):
            lo, hi = low_block[r * 8 : r * 8 + 8, :], top_block[r * 8 : r * 8 + 8, :]
            low = low + jnp.where((lo <= b) & (b < hi), lows[r], 0.0)
        lowest.append(jnp.sum(low, axis=0, keepdims=True))

    n_of, spot = iota((32, 256), 1), iota((32, 256), 0)
    in_group = lax.shift_right_logical(n_of, 3) == spot
    in_tile = lax.shift_right_logical(n_of, 6) * 8 + (n_of & 7) == spot
    n_of, spot = iota((256, 128), 0), iota((256, 128), 1) & 7
    by_last = jnp.where((n_of & 7) == spot, 1.0, 0.0).astype(bf)
    by_octant = jnp.where((lax.shift_right_logical(n_of, 3) & 7) == spot, 1.0, 0.0).astype(bf)

    def fold(values, rows_of, lanes_of):
        high = jnp.floor(values * (1.0 / 64.0))
        out = jnp.zeros((32, 128), f32)
        for part, scale in ((high, 64.0), (values - 64.0 * high, 1.0)):
            spread = jnp.where(rows_of, jnp.broadcast_to(part, (32, 256)), 0.0).astype(bf)
            out = out + scale * jnp.dot(spread, lanes_of, preferred_element_type=f32)
        return out

    dst = (sums[:, 0:256] + begin[:, 0:256])[0:1].astype(f32)
    code = (sums[:, 512:768] * 8 + source[...])[0:1].astype(f32)
    dst_lined = (sums[:, 256:512] + begin[:, 256:512])[0:1].astype(f32)
    table = [
        fold(code, in_group, by_last),
        fold(dst_lined, in_group, by_last),
        fold(lined[0:1].astype(f32), in_group, by_last),
        fold(widest(lined, (1, 2, 4))[0:1].astype(f32), in_group, by_last),
        fold(dst, in_tile, by_octant),
        fold(number[0:1].astype(f32), in_tile, by_octant),
        fold(widest(number, (8, 16, 32))[0:1].astype(f32), in_tile, by_octant),
        jnp.broadcast_to(top_block[127:128, :], (32, 128)),
    ]
    for j in range(3):
        table.append(fold(jnp.concatenate(lowest[2 * j : 2 * j + 2], axis=1), in_group, by_last))
    section = lax.shift_right_logical(iota((32, 128), 1), 3)
    final = jnp.zeros((32, 128), f32)
    for n, values in enumerate(table):
        final = jnp.where(section == n, values, final)
    tab[...] = final.astype(jnp.int32)
    stores[4].start()

    for c in copies + stores:
        c.wait()


def exchange_kernel(t, heat, t_all, heat_all, ssem, rsem, csem, dsem):
    greet()
    copies = []
    for n, (dx, dy) in enumerate(SIDES):
        sx, sy, rx, ry = span(dx, True), span(dy, True), span(dx, False), span(dy, False)
        copies.append(remote(t.at[sx, sy], t_all.at[rx, ry], ssem.at[n], rsem.at[n], dx, dy))
        copies.append(remote(heat.at[sx, sy], heat_all.at[rx, ry], csem.at[n], dsem.at[n], dx, dy))
    for c in copies:
        c.start()
    for c in copies:
        c.wait()


def pack_rows(tab, rows, packed):
    part = lax.shift_right_logical(iota((8, 128), 1), 4)

    def step(i, carry):
        widest = tab[i, 24]

        def move(u, chunks):
            code, dst = tab[i, u], tab[i, 8 + u]
            src = lax.shift_right_logical(code, 3)
            mine = part == (code & 7)
            for k in chunks:
                packed[pl.ds(dst + 8 * k, 8), :] = jnp.where(mine, rows[pl.ds(src + 8 * k, 8), :], 0.0)

        for less, most in zip(FAST, FAST[1:]):

            @pl.when((widest > less * 8) & (widest <= most * 8))
            def _(most=most):
                for u in range(GROUP):
                    move(u, range(most))

        @pl.when(widest > FAST[-1] * 8)
        def _():
            def one(u, carry):
                def inner(k, carry):
                    move(u, (k,))
                    return carry

                return lax.fori_loop(0, (tab[i, 16 + u] + 7) // 8, inner, carry)

            lax.fori_loop(0, GROUP, one, 0)

        return carry

    lax.fori_loop(0, 256 // GROUP, step, 0)


def over_tiles(tab, chunk, acc):
    count = acc.shape[0]

    def put(tile, lanes):
        for n in range(count):
            acc[n, pl.ds(pl.multiple_of(tile * 8, 8), 8), :] = lanes[n]

    def step(tile, carry):
        widest = tab[tile, 48]

        for less, most in zip(FAST, FAST[1:]):

            @pl.when((widest > less * 8) & (widest <= most * 8))
            def _(most=most):
                chains = [None] * 4
                for o in range(8):
                    base = tab[tile, 32 + o]
                    for k in range(most):
                        at = (o * most + k) % 4
                        new = chunk(tile, o, base + 8 * k, k)
                        old = chains[at]
                        chains[at] = new if old is None else [p + q for p, q in zip(old, new)]
                put(tile, [(a + b) + (c + d) for a, b, c, d in zip(*chains)])

        @pl.when(widest > FAST[-1] * 8)
        def _():
            def per(o, lanes):
                base = tab[tile, 32 + o]

                def inner(k, lanes):
                    return tuple(p + q for p, q in zip(lanes, chunk(tile, o, base + 8 * k, k)))

                return lax.fori_loop(0, (tab[tile, 40 + o] + 7) // 8, inner, lanes)

            put(tile, lax.fori_loop(0, 8, per, (jnp.zeros((8, 128), f32),) * count))

        return carry

    lax.fori_loop(0, TILES, step, 0)


def of_column(acc, n, col):
    total = acc[n, pl.ds(col * 64, 8, stride=8), :]
    for k in range(1, 8):
        total = total + acc[n, pl.ds(col * 64 + k, 8, stride=8), :]
    return total


def around(low):
    return [low + (dx * 4 + dy) * COLUMN + dz for dx in (0, 1) for dy in (0, 1) for dz in (0, 1)]


def matcher(key):
    sub = iota((8, 128), 0)

    def match(tile, octant, k):
        return key[pl.ds(tile, 8, stride=0), :] == sub + (octant * RANK_KEY + k * 8)

    return match


def slope_of(tot):
    return wide(0.1875 + 0.625 * lax.rsqrt(jnp.sum(tot, axis=1, keepdims=True)))


def density_kernel(
    tab_h, rows_h, halo_h, cbuf_h, pos_h, cnt_h, key_h, w_h, tl_h, jf_h,
    tab, rows, halo, cbuf, pos, cnt, key, jf, packed, ti, tl, acc, wb, own, last, insem, outsem, wsem,
):
    loads = [
        pltpu.make_async_copy(src, dst, insem.at[n])
        for n, (src, dst) in enumerate(
            (
                (tab_h, tab), (rows_h, rows.at[0:512]), (halo_h, halo), (cbuf_h, cbuf),
                (pos_h, pos), (cnt_h, cnt), (key_h, key),
            )
        )
    ]
    for c in loads:
        c.start()
    for col in range(16):
        for n in range(4):
            empty = jnp.full((8, 128), FAR if n < 3 else -3.0 * FAR * FAR, f32)
            jf[n, col * COLUMN : col * COLUMN + 8, :] = empty
            jf[n, col * COLUMN + 16 : col * COLUMN + 24, :] = empty
    for c in loads:
        c.wait()

    def features(hx, hy, xyz, live):
        first = (hx * 4 + hy) * COLUMN + 8
        out = features_of(hx, hy, xyz, live)
        for n in range(3):
            jf[n, first : first + 8, :] = out[n]
        jf[3, first : first + 8, :] = -(out[0] * out[0] + out[1] * out[1] + out[2] * out[2])

    for n, (dx, dy) in enumerate(SIDES):
        for hx in range(4)[span(dx, False)]:
            for hy in range(4)[span(dy, False)]:
                sx = hx - 1 if dx == 0 else (1 if dx > 0 else 0)
                sy = hy - 1 if dy == 0 else (1 if dy > 0 else 0)
                live = alive_of(cbuf[n, sx, pl.ds(sy, 8, stride=0), :])
                features(hx, hy, [halo[m, hx, hy] for m in range(3)], live)
    for x in range(2):
        for y in range(2):
            live = alive_of(cnt[x, pl.ds(y, 8, stride=0), :])
            features(x + 1, y + 1, [pos[m, x, y] for m in range(3)], live)
    places = pltpu.make_async_copy(jf.at[0:3], jf_h, outsem.at[1])
    places.start()
    pack_rows(tab, rows, packed)
    count = tab[0, 56]
    feature = iota((8, 128), 1) & 15
    masks = [(feature == n) | (feature == n + 3) | (feature == n + 6) for n in range(3)]

    def own_rows(b):
        out = []
        for k in range(PER):
            value = packed[pl.ds(pl.multiple_of(b * BLOCK + 8 * k, 8), 8), :]
            x, y, z = (wide(jnp.sum(jnp.where(m, value, 0.0), axis=1, keepdims=True)) for m in masks)
            out += [x + x, y + y, z + z, 1.0 - (x * x + y * y + z * z)]
        return out

    def keep(blocks):
        for u, values in enumerate(blocks):
            for n, value in enumerate(values):
                own[u, n] = value

    def settle(i, tots):
        for u in range(STEP):
            b = i * STEP + u
            for k in range(PER):
                t = slope_of(tots[u][k])
                ti[pl.ds(pl.multiple_of(b * BLOCK + 8 * k, 8), 8), :] = t
                wb[b, (8 * PER + k) * 8 : (8 * PER + k) * 8 + 8, :] = t

    def step(i, carry):
        tots = [[last[u, k] for k in range(PER)] for u in range(STEP)]
        ahead = [own_rows(jnp.minimum((i + 1) * STEP + u, BLOCKS - 1)) for u in range(STEP)]
        new = []
        for u in range(STEP):
            b = i * STEP + u
            mine = [[own[u, 4 * k + n] for n in range(4)] for k in range(PER)]
            tot = [None] * PER
            for n, tile in enumerate(around(tab[i & 31, 64 + (lax.shift_right_logical(i, 5) * 8 + u)])):
                xj, yj, zj, bj = (jf[m, pl.ds(tile, 8, stride=0), :] for m in range(4))
                for k in range(PER):
                    x, y, z, a = mine[k]
                    w = jnp.maximum((a + bj) + (x * xj + y * yj + z * zj), 0.0)
                    wb[b, (n * PER + k) * 8 : (n * PER + k) * 8 + 8, :] = w
                    cube = w * w * w
                    tot[k] = cube if tot[k] is None else tot[k] + cube
            new.append(tot)
        settle(jnp.maximum(i - 1, 0), tots)
        keep(ahead)
        for u in range(STEP):
            for k in range(PER):
                last[u, k] = new[u][k]
        return carry

    def saved(g):
        part = pl.ds(g * CHUNK, CHUNK)
        return pltpu.make_async_copy(wb.at[part], w_h.at[part], wsem.at[g])

    steps = (count + STEP - 1) // STEP
    groups = (count + CHUNK - 1) // CHUNK
    per = CHUNK // STEP

    def group(g, carry):
        lax.fori_loop(g * per, jnp.minimum(g * per + per, steps), step, 0)

        @pl.when(g > 0)
        def _():
            saved(g - 1).start()

        return carry

    keep([own_rows(u) for u in range(STEP)])
    last[...] = jnp.ones_like(last)
    lax.fori_loop(0, groups, group, 0)
    settle(steps - 1, [[last[u, k] for k in range(PER)] for u in range(STEP)])
    saved(groups - 1).start()

    match = matcher(key)

    def chunk(tile, octant, row, k):
        return [jnp.where(match(tile, octant, k), ti[pl.ds(row, 8), :], 0.0)]

    over_tiles(tab, chunk, acc)
    for col in range(4):
        tl[col * 8 : col * 8 + 8, :] = of_column(acc, 0, col)
    lanes_out = pltpu.make_async_copy(tl, tl_h, outsem.at[0])
    lanes_out.start()

    def drain(g, carry):
        saved(g).wait()
        return carry

    lax.fori_loop(0, groups, drain, 0)
    lanes_out.wait()
    places.wait()


def diffuse(heat, out, old, new):
    for x in range(12):
        for y in range(4):
            old[x, y * 3 : y * 3 + 8, :] = heat[x // 3, y, x % 3]
    lane = iota((8, 128), 1)
    for s in range(3):
        for x in range(s + 1, 11 - s):
            for r in (1, 9) if s == 0 else (s + 1,):
                t = old[x, r : r + 8, :]
                near = [old[x - 1, r : r + 8, :], old[x + 1, r : r + 8, :], old[x, r - 1 : r + 7, :], old[x, r + 1 : r + 9, :]]
                q = t * t
                side = near[0] * near[0] + near[1] * near[1] + near[2] * near[2] + near[3] * near[3] - 4.0 * q
                up = jnp.where(lane < 23, pltpu.roll(q, 127, 1) - q, 0.0)
                t = t + 0.025 * (side + (up - pltpu.roll(up, 1, 1)))
                if s < 2:
                    new[x, r : r + 8, :] = t
                else:
                    out[x - 3, :, :] = t[0:6, 0:24]
        old, new = new, old


def force_kernel(
    tab_h, w_h, jf_h, t_all_h, tl_h, key_h, pv_h, heat_all_h, heat_h, vel_h, temp_h,
    tab, wb, jf, tj, tl, key, pv, heat, own, vel, temp, fg, fx, fy, fz, acc, last, old, new, insem, outsem, wsem,
):
    def loaded(g):
        part = pl.ds(g * CHUNK, CHUNK)
        return pltpu.make_async_copy(w_h.at[part], wb.at[part], wsem.at[g])

    loads = [
        pltpu.make_async_copy(src, dst, insem.at[n])
        for n, (src, dst) in enumerate(
            (
                (tab_h, tab), (heat_all_h, heat), (heat_h, own), (t_all_h, tj.at[:, 8:16]),
                (tl_h, tl), (jf_h, jf), (key_h, key), (pv_h, pv),
            )
        )
    ]
    for c in loads:
        c.start()
    loaded(0).start()
    loads[0].wait()
    count = tab[0, 56]
    groups = (count + CHUNK - 1) // CHUNK

    def fetch(g, carry):
        loaded(g).start()
        return carry

    lax.fori_loop(1, groups, fetch, 0)
    none = jnp.zeros((8, 128), f32)
    for col in range(16):
        tj[col, 0:8, :] = none
        tj[col, 16:24, :] = none
    for c in loads[1:3]:
        c.wait()
    for x in range(2):
        for y in range(2):
            heat[x + 1, y + 1] = own[x, y]
    diffuse(heat, temp, old, new)
    warm = pltpu.make_async_copy(temp, temp_h, outsem.at[1])
    warm.start()
    for c in loads[3:]:
        c.wait()
    for col in range(4):
        tj[(col // 2 + 1) * 4 + col % 2 + 1, 8:16, :] = tl[col * 8 : col * 8 + 8, :]
    sums = (fg, fx, fy, fz)

    def settle(i):
        for u in range(STEP):
            row = (i * STEP + u) * BLOCK
            for k in range(PER):
                for n, f in enumerate(sums):
                    at = pl.ds(pl.multiple_of(row + 8 * k, 8), 8)
                    f[at, :] = wide(jnp.sum(last[u, 4 * k + n], axis=1, keepdims=True))

    def step(i, carry):
        settle(jnp.maximum(i - 1, 0))
        new = []
        for u in range(STEP):
            b = i * STEP + u
            t_own = [wb[b, (8 * PER + k) * 8 : (8 * PER + k) * 8 + 8, :] for k in range(PER)]
            tot = [None] * (4 * PER)
            for n, tile in enumerate(around(tab[i & 31, 64 + (lax.shift_right_logical(i, 5) * 8 + u)])):
                other = [jf[m, pl.ds(tile, 8, stride=0), :] for m in range(3)]
                t_other = tj.at[...].reshape(16 * COLUMN, 128)[pl.ds(tile, 8, stride=0), :]
                for k in range(PER):
                    w = wb[b, (n * PER + k) * 8 : (n * PER + k) * 8 + 8, :]
                    g = (w * w) * ((t_own[k] + t_other) - w)
                    for m, p in enumerate((g, g * other[0], g * other[1], g * other[2])):
                        at = 4 * k + m
                        tot[at] = p if tot[at] is None else tot[at] + p
            new.append(tot)
        for u in range(STEP):
            for n in range(4 * PER):
                last[u, n] = new[u][n]
        return carry

    steps = (count + STEP - 1) // STEP
    per = CHUNK // STEP

    def group(g, carry):
        loaded(g).wait()
        return lax.fori_loop(g * per, jnp.minimum(g * per + per, steps), step, carry)

    last[...] = jnp.zeros_like(last)
    lax.fori_loop(0, groups, group, 0)
    settle(steps - 1)

    match = matcher(key)

    def chunk(tile, octant, row, k):
        hit = match(tile, octant, k)
        return [jnp.where(hit, f[pl.ds(row, 8), :], 0.0) for f in sums]

    over_tiles(tab, chunk, acc)
    for col in range(4):
        total = [of_column(acc, n, col) for n in range(4)]
        tiles = slice(col * 8, col * 8 + 8)
        at = ((col // 2 + 1) * 4 + col % 2 + 1) * COLUMN + 8
        live = key[tiles, :] >= 0
        for n in range(3):
            pull = jf[n, at : at + 8, :] * total[0] - total[n + 1]
            vel[n, tiles, :] = jnp.where(live, pv[n, tiles, :] + pull * (-2.4 / ROOT), 0.0)
    out = pltpu.make_async_copy(vel, vel_h, outsem.at[0])
    out.start()
    out.wait()
    warm.wait()


ANY = pl.BlockSpec(memory_space=pltpu.HBM)
LOCAL = pltpu.CompilerParams(vmem_limit_bytes=67043328)


def shape(*dims, dtype=f32):
    return jax.ShapeDtypeStruct(dims, dtype)


def vmem(like):
    return pltpu.VMEM(like.shape, like.dtype)


def meeting(n):
    return pltpu.CompilerParams(collective_id=n, has_side_effects=True, vmem_limit_bytes=67043328)


def density_scratch():
    i32, dma = jnp.int32, pltpu.SemaphoreType.DMA
    return [
        pltpu.SMEM((32, 128), i32),
        pltpu.VMEM((1024, 128), f32),
        pltpu.VMEM((3, 4, 4, 8, 128), f32),
        pltpu.VMEM((8, 2, 2, 8), i32),
        pltpu.VMEM((3, 2, 2, 8, 128), f32),
        pltpu.VMEM((2, 2, 8), i32),
        pltpu.VMEM((TILES, 128), i32),
        pltpu.VMEM((4, 16 * COLUMN, 128), f32),
        pltpu.VMEM((ROWS, 128), f32),
        pltpu.VMEM((ROWS, 128), f32),
        pltpu.VMEM((TILES, 128), f32),
        pltpu.VMEM((1, TILES * 8, 128), f32),
        pltpu.VMEM((BLOCKS, WIDE, 128), f32),
        pltpu.VMEM((STEP, 4 * PER, 8, 128), f32),
        pltpu.VMEM((STEP, PER, 8, 128), f32),
        dma((7,)),
        dma((2,)),
        dma((BLOCKS // CHUNK,)),
    ]


def force_scratch():
    dma = pltpu.SemaphoreType.DMA
    return [
        pltpu.SMEM((32, 128), jnp.int32),
        pltpu.VMEM((BLOCKS, WIDE, 128), f32),
        pltpu.VMEM((3, 16 * COLUMN, 128), f32),
        pltpu.VMEM((16, COLUMN, 128), f32),
        pltpu.VMEM((TILES, 128), f32),
        pltpu.VMEM((TILES, 128), jnp.int32),
        pltpu.VMEM((3, TILES, 128), f32),
        pltpu.VMEM((4, 4, 3, 8, 128), f32),
        pltpu.VMEM((2, 2, 3, 8, 128), f32),
        pltpu.VMEM((3, TILES, 128), f32),
        pltpu.VMEM((6, 6, 24), f32),
        *(pltpu.VMEM((ROWS, 128), f32),) * 4,
        pltpu.VMEM((4, TILES * 8, 128), f32),
        pltpu.VMEM((STEP, 4 * PER, 8, 128), f32),
        *(pltpu.VMEM((12, 24, 128), f32),) * 2,
        dma((8,)),
        dma((2,)),
        dma((BLOCKS // CHUNK,)),
    ]


def local(positions, velocities, kicks, counts, subcell, electron_temp, laser_flux):
    *zeroone, source = static_tables()
    upper = np.triu(np.ones((128, 128)))
    bf = jnp.bfloat16
    i32 = jnp.int32
    dma = pltpu.SemaphoreType.DMA
    around8 = [dma((8,))] * 4
    tiles = shape(3, 2, 2, 8, 128)
    outs = (
        shape(TILES, 128, dtype=i32),
        shape(32, 128, dtype=i32),
        shape(2, 2, 3, 8, 128),
        shape(3, TILES, 128),
        shape(512, 128),
    )
    halo = shape(3, 4, 4, 8, 128)
    cbuf = shape(8, 2, 2, 8, dtype=i32)
    halo_all, counts_all, key, tab, heat, pv, rows = pl.pallas_call(
        gather_kernel,
        name="gather",
        out_shape=(halo, cbuf, *outs),
        in_specs=[ANY] * 12,
        out_specs=(ANY,) * 7,
        scratch_shapes=[
            *(vmem(tiles),) * 3,
            pltpu.VMEM((2, 2, 8), i32),
            pltpu.VMEM((2, 2, 8, 128), i32),
            pltpu.VMEM((6, 6, 24), f32),
            pltpu.SMEM((6, 6), f32),
            pltpu.VMEM((128, 128), bf),
            *(pltpu.VMEM(m.shape, bf) for m in zeroone),
            pltpu.VMEM(source.shape, i32),
            *(vmem(o) for o in outs),
            pltpu.VMEM((256, 128), f32),
            pltpu.VMEM((TILES, 128), i32),
            pltpu.VMEM((8, 16, 128), f32),
            dma((12,)),
            dma((5,)),
            *around8,
        ],
        compiler_params=meeting(0),
    )(
        positions, velocities, kicks, counts, subcell, electron_temp, laser_flux,
        *(jnp.asarray(m, bf) for m in (upper, *zeroone)), jnp.asarray(source),
    )
    row = shape(ROWS, 128)
    saved = shape(BLOCKS, WIDE, 128)
    flat = shape(TILES, 128)
    corner = shape(3, 16 * COLUMN, 128)
    w, tl, jf = pl.pallas_call(
        density_kernel,
        name="density",
        out_shape=(saved, flat, corner),
        in_specs=[ANY] * 7,
        out_specs=(ANY,) * 3,
        scratch_shapes=density_scratch(),
        compiler_params=LOCAL,
    )(tab, rows, halo_all, counts_all, positions, counts, key)
    t_all, heat_all = pl.pallas_call(
        exchange_kernel,
        name="exchange",
        out_shape=(shape(4, 4, 8, 128), shape(4, 4, 3, 8, 128)),
        in_specs=[ANY] * 2,
        out_specs=(ANY,) * 2,
        scratch_shapes=around8,
        compiler_params=meeting(1),
    )(tl.reshape(2, 2, 8, 128), heat)
    vel, temp = pl.pallas_call(
        force_kernel,
        name="force",
        out_shape=(outs[3], shape(6, 6, 24)),
        in_specs=[ANY] * 9,
        out_specs=(ANY,) * 2,
        scratch_shapes=force_scratch(),
        compiler_params=LOCAL,
    )(tab, w, jf, t_all.reshape(16, 8, 128), tl, key, pv, heat_all, heat)
    return (vel.reshape(3, 2, 2, 8, 128), temp)


def solution(mesh):
    in_specs = (
        P(None, "gx", "gy", None, None),
        P(None, "gx", "gy", None, None),
        P(None, "gx", "gy", None, None),
        P("gx", "gy", None),
        P("gx", "gy", None, None),
        P("gx", "gy", None),
        P("gx", "gy"),
    )
    out_specs = (P(None, "gx", "gy", None, None), P("gx", "gy", None))
    return jax.shard_map(local, mesh=mesh, in_specs=in_specs, out_specs=out_specs, check_vma=False)
```
